32 devices in a mesh: streams: 8 (over z, x), tm: 4 (over y, core).
Axes of the slice: x: 2, y: 2, z: 4, core: 2. Of those that a mesh axis runs over, the one named last changes fastest.
Arguments:
- signal: float32 [2, 2097152], P(None, ('streams', 'tm')), parts along dimension 1, may hold values from -6 to 6
- coarse_taps: float32 [16, 64], replicated, may hold values from -1.5 to 1.5
- fine_taps: float32 [12, 512], replicated, may hold values from -1.8 to 1.8
Outputs:
- channelized: float32 [2, 64, 64, 512], P(None, 'tm', 'streams'), parts along dimension 2
The draws below stay inside these ranges and needn't reach their ends.
There are 8 independent parts, one for each index of `streams`. The reference program is written for one: setup_inputs(seed, part) draws one part's arguments, and reference() takes and returns one part's arrays. A program takes and returns all parts, laid end to end along the dimension named above; an argument that names none is the same for every part. Nothing has to cross between parts.
All inputs are finite; a program needn't handle non-finite values.
Results may differ from the reference program's by a relative error of at most 0.00007.
Values sent between devices are 32-bit elements; how exact they have to be, the bound alone decides.
No kernel may reach another device: no remote copies, remote signals or barrier semaphores. Data moves between devices by JAX's collectives and lax.ppermute only.
A program may use at most 320 MiB of HBM per device.

```python
import math
import jax
import jax.numpy as jnp
from jax import lax

CHANNELS = 64
FINE = 512
TAPS = 16
FINE_TAPS = 12
SAMPLES = 262144
FRAMES = 4096
FINE_FRAMES = 8


def steps_of(rng, dims, cuts, low, largest):
    def one(dim, blocks):
        steps = jax.random.uniform(jax.random.fold_in(jax.random.fold_in(rng, 6), dim), (blocks,), jnp.float32, low / len(cuts), largest / len(cuts))
        return jnp.repeat(jnp.exp(steps), dims[dim] // blocks).reshape((-1,) + (1,) * (len(dims) - dim - 1))

    factor_of = one(*cuts[0])
    for cut in cuts[1:]:
        factor_of = factor_of * one(*cut)
    return factor_of


def noise(own_key, dims, deviation, most, cuts=(), kind=jnp.bfloat16):
    loudness = steps_of(own_key, dims, cuts, -0.22, 0.18) if cuts else 1.0
    result = jax.random.normal(own_key, dims, jnp.float32) * deviation * loudness
    return jnp.minimum(jnp.maximum(result, -most), most).astype(kind)


def setup_inputs(seed: int = 0, part: int = 0) -> dict:
    keys = jax.random.split(jax.random.key(seed), 4)
    own_keys = jax.random.split(jax.random.fold_in(keys[3], part), 4)
    signal = noise(own_keys[0], (2, SAMPLES), 1.0, 6.0, ((1, 4),), jnp.float32)
    coarse_taps = noise(keys[1], (TAPS, CHANNELS), 0.25, 1.5, (), jnp.float32)
    fine_taps = noise(keys[2], (FINE_TAPS, FINE), 0.3, 1.8, (), jnp.float32)
    return dict(signal=signal, coarse_taps=coarse_taps, fine_taps=fine_taps)


def tables(points):
    counter = jnp.arange(points, dtype=jnp.int32)
    product = counter[:, None] * counter[None, :] % points
    angle = product.astype(jnp.float32) * (2.0 * math.pi / points)
    return (jnp.cos(angle), jnp.sin(angle))

def spectrum_last(real_part, imag_part, points):
    cosine_table, sine_table = tables(points)
    factor = 1.0 / math.sqrt(points)
    highest = lax.Precision.HIGHEST
    out_real = (jnp.matmul(real_part, cosine_table, precision=highest) + jnp.matmul(imag_part, sine_table, precision=highest)) * factor
    out_imag = (jnp.matmul(imag_part, cosine_table, precision=highest) - jnp.matmul(real_part, sine_table, precision=highest)) * factor
    return jnp.stack([out_real, out_imag])

def reference(signal, coarse_taps, fine_taps):
    framed = signal.reshape(2, FRAMES, CHANNELS)
    padded = jnp.pad(framed, ((0, 0), (TAPS - 1, 0), (0, 0)))
    branches = jnp.zeros((2, FRAMES, CHANNELS), jnp.float32)
    for tap_index in range(TAPS):
        offset = TAPS - 1 - tap_index
        branches = branches + coarse_taps[tap_index] * padded[:, offset:offset + FRAMES, :]
    coarse = spectrum_last(branches[0], branches[1], CHANNELS)
    coarse = jnp.transpose(coarse, (0, 2, 1)).reshape(2, CHANNELS, FINE_FRAMES, FINE)
    padded_fine = jnp.pad(coarse, ((0, 0), (0, 0), (FINE_TAPS - 1, 0), (0, 0)))
    fine_branches = jnp.zeros((2, CHANNELS, FINE_FRAMES, FINE), jnp.float32)
    for tap_index in range(FINE_TAPS):
        offset = FINE_TAPS - 1 - tap_index
        fine_branches = fine_branches + fine_taps[tap_index] * padded_fine[:, :, offset:offset + FINE_FRAMES, :]
    return spectrum_last(fine_branches[0], fine_branches[1], FINE)
```

```python
import math

import jax
import jax.numpy as jnp
import numpy as np
from jax import lax
from jax.experimental import pallas as pl
from jax.experimental.pallas import tpu as pltpu
from jax.sharding import PartitionSpec as P

LANES = 128
F32, BF16 = jnp.float32, jnp.bfloat16


def split_table(table):
    high = np.asarray(table, np.float32).astype(jnp.bfloat16)
    low = (np.asarray(table, np.float64) - high.astype(np.float64)).astype(np.float32).astype(jnp.bfloat16)
    return high, low


def complex_table(turns, points, factor):
    angle = (turns % points) * (2.0 * math.pi / points)
    return np.cos(angle) * factor, -np.sin(angle) * factor


def coarse_table(channels, groups):
    halves, per = LANES // channels, channels // groups
    k, p = np.arange(channels), np.arange(channels)
    real, imag = complex_table(k[:, None] * p[None, :], channels, 1.0 / math.sqrt(channels))
    table = np.zeros((groups, 2, halves, per, 2, halves, channels))
    real, imag = real.reshape(groups, per, channels), imag.reshape(groups, per, channels)
    for half in range(halves):
        table[:, 0, half, :, 0, half] = real
        table[:, 0, half, :, 1, half] = -imag
        table[:, 1, half, :, 0, half] = imag
        table[:, 1, half, :, 1, half] = real
    return table.reshape(2 * LANES, 2 * LANES)


def fine_tables(fine):
    radix = fine // LANES
    i = np.arange(LANES)
    real, imag = complex_table(i[:, None] * i[None, :], LANES, 1.0 / math.sqrt(fine))
    table = np.block([[real, imag], [-imag, real]])
    real, imag = complex_table(np.arange(radix)[:, None] * i[None, :], fine, 1.0)
    return table, np.stack([real, imag], axis=1).astype(np.float32)


def split_value(value):
    high = value.astype(BF16)
    return high, (value - high.astype(F32)).astype(BF16)


def dot_nt(left, right):
    return lax.dot_general(left, right, (((1,), (1,)), ((), ())), preferred_element_type=F32)


def dot_nn(left, right):
    return lax.dot_general(left, right, (((1,), (0,)), ((), ())), preferred_element_type=F32)


VMEM = pl.BlockSpec(memory_space=pltpu.VMEM)
ANY = pl.BlockSpec(memory_space=pl.ANY)
PARAMS = pltpu.CompilerParams(vmem_limit_bytes=24 * 1024 * 1024)


def in_vmem(value):
    return pltpu.with_memory_space_constraint(value, pltpu.VMEM)


def coarse_kernel(axis, groups, x_hbm, taps_ref, high_ref, low_ref, *rest):
    outs, (xs, ys, bs, sem) = rest[:groups], rest[groups:]
    rows = x_hbm.shape[0]
    channels = taps_ref.shape[1]
    taps_count = taps_ref.shape[0]
    pad = 16
    copy = pltpu.make_async_copy(x_hbm, xs.at[pl.ds(pad, rows)], sem)
    copy.start()
    zeros = jnp.zeros((pad, LANES), F32)
    xs[:pad] = zeros
    xs[pad + rows :] = zeros
    taps = taps_ref[...]
    taps = jnp.concatenate([taps, taps], axis=1)
    me = lax.axis_index(axis)
    span = 2 * LANES // groups
    picks = [pl.multiple_of((me ^ step) * span, span) for step in range(groups)]
    high = jnp.concatenate([high_ref[pl.ds(pick, span), :] for pick in picks], axis=0)
    low = jnp.concatenate([low_ref[pl.ds(pick, span), :] for pick in picks], axis=0)
    copy.wait()

    lane = lax.broadcasted_iota(jnp.int32, (1, LANES), 1)
    lower = lane < channels
    total = rows + pad
    ys[:pad] = zeros
    block = 80
    for base in range(0, total, block):
        now = xs[pad + base : pad + base + block]
        before = xs[pad + base - 2 : pad + base + block - 2]
        ys[pad + base : pad + base + block] = pltpu.roll(jnp.where(lower, now, before), channels, 1)
    for base in range(0, total, block):
        summed = None
        for parity, source in ((0, xs), (1, ys)):
            for shift in range(taps_count // 4):
                start = pad + base - 2 * shift - 8
                piece = source[start : start + block + 8]
                near = taps[2 * shift + parity][None, :]
                far = taps[2 * (shift + 4) + parity][None, :]
                term = piece[8:] * near + piece[:block] * far
                summed = term if summed is None else summed + term
        bs[base : base + block] = summed

    half_rows = rows // 2
    for frame in range(2):
        parts = []
        for a in range(2):
            pair = [bs[pl.ds(frame * half_rows + 2 * a + part, LANES, stride=4), :] for part in range(2)]
            parts.append(jnp.concatenate(pair, axis=1))
        bh, bl = split_value(jnp.concatenate(parts, axis=0))
        result = dot_nt(high, bh) + dot_nt(low, bh) + dot_nt(high, bl)
        for step in range(groups):
            for a in range(2):
                at = (frame * 2 + a) * span
                outs[step][at : at + span] = result[step * span : (step + 1) * span, a * LANES : (a + 1) * LANES]
    parts = []
    for a in range(2):
        pair = [bs[pl.ds(rows + 2 * a + part, 4, stride=4), :] for part in range(2)]
        parts.append(jnp.concatenate(pair, axis=1))
    bh, bl = split_value(jnp.concatenate(parts, axis=0))
    tail = dot_nt(bh, high) + dot_nt(bh, low) + dot_nt(bl, high)
    for step in range(groups):
        at = step * span // LANES * LANES
        outs[step][4 * span : 4 * span + 8] = tail[:, at : at + LANES]


def coarse_section(signal, coarse_taps, axis, groups):
    length = signal.shape[1]
    channels = coarse_taps.shape[1]
    chunks = length // LANES
    rows = signal.reshape(2, chunks, LANES).transpose(1, 0, 2).reshape(2 * chunks, LANES)
    high, low = split_table(coarse_table(channels, groups))
    span = 2 * LANES // groups
    kernel = lambda *refs: coarse_kernel(axis, groups, *refs)
    return pl.pallas_call(
        kernel,
        out_shape=[pltpu.VMEM((4 * span + 8, LANES), F32)] * groups,
        in_specs=[ANY, VMEM, VMEM, VMEM],
        out_specs=[VMEM] * groups,
        scratch_shapes=[
            pltpu.VMEM((2 * chunks + 32, LANES), F32),
            pltpu.VMEM((2 * chunks + 32, LANES), F32),
            pltpu.VMEM((2 * chunks + 16, LANES), F32),
            pltpu.SemaphoreType.DMA,
        ],
        compiler_params=PARAMS,
        name="coarse",
    )(rows, coarse_taps, jnp.asarray(high), jnp.asarray(low))


def fine_kernel(axis, groups, taps_ref, high_ref, low_ref, turn_ref, *rest):
    pieces, out_ref, (xs, yh, yl, zs) = rest[:groups], rest[groups], rest[groups + 1 :]
    span = 2 * LANES // groups
    per = span // 4
    frames = 2 * groups
    taps_count = taps_ref.shape[1]
    me = lax.axis_index(axis)
    for step in range(groups):
        owner = me ^ step
        for frame in range(2):
            for a in range(2):
                at = (frame * 2 + a) * span
                xs[2 * owner + frame, a] = pieces[step][at : at + span]
    lane = lax.broadcasted_iota(jnp.int32, (1, LANES), 1)
    for step in range(groups):
        owner = me ^ step
        tail = jnp.transpose(pieces[step][4 * span : 4 * span + 8])
        at = step * span % LANES
        tail = tail[at : at + span]
        for a in range(2):
            into = xs[2 * owner + 2, a, :, 0:4]
            xs[2 * owner + 2, a, :, 0:4] = into + tail[:, 4 * a : 4 * a + 4]
    for a in range(2):
        for h in range(2):
            phase = 2 * a + h
            for part in range(2):
                at = (2 * part + h) * per
                for m in range(frames):
                    summed = None
                    for j in range(min(m + 1, taps_count)):
                        term = xs[m - j, a, at : at + per] * taps_ref[phase, j : j + 1]
                        summed = term if summed is None else summed + term
                    high, low = split_value(summed)
                    yh[phase, m * per : (m + 1) * per, part * LANES : (part + 1) * LANES] = high
                    yl[phase, m * per : (m + 1) * per, part * LANES : (part + 1) * LANES] = low
    height = 4 * frames * per
    left, right = yh[...].reshape(height, 2 * LANES), yl[...].reshape(height, 2 * LANES)
    high, low = high_ref[...], low_ref[...]
    zs[...] = (dot_nn(left, high) + dot_nn(right, high) + dot_nn(left, low)).reshape(4, frames * per, 2 * LANES)
    size = min(8, per)
    blocks = frames // 8
    for at in range(0, frames * per, 8):
        z = []
        for phase in range(4):
            real, imag = zs[phase, at : at + 8, :LANES], zs[phase, at : at + 8, LANES:]
            if phase:
                c, s = turn_ref[phase, 0:1], turn_ref[phase, 1:2]
                real, imag = real * c - imag * s, real * s + imag * c
            z.append((real, imag))
        (ar, ai), (br, bi), (cr, ci), (dr, di) = z
        pr, pi, qr, qi = ar + cr, ai + ci, ar - cr, ai - ci
        ur, ui, vr, vi = br + dr, bi + di, br - dr, bi - di
        reals = (pr + ur, qr + vi, pr - ur, qr - vi)
        imags = (pi + ui, qi - vr, pi - ui, qi + vr)
        for part, values in enumerate((reals, imags)):
            for r, value in enumerate(values):
                for inner in range(0, 8, size):
                    m, k = divmod(at + inner, per)
                    row = (((part * per + k) * blocks + m // 8) * 4 + r) * 8 + m % 8
                    out_ref[pl.ds(row, size, stride=32 * blocks), :] = value[inner : inner + size]


def fine_section(pieces, fine_taps, axis, groups):
    fine = fine_taps.shape[1]
    taps_count = fine_taps.shape[0]
    span = 2 * LANES // groups
    per, frames = span // 4, 2 * groups
    taps = fine_taps.reshape(taps_count, LANES, fine // LANES).transpose(2, 0, 1)
    table, turns = fine_tables(fine)
    high, low = split_table(table)
    kernel = lambda *refs: fine_kernel(axis, groups, *refs)
    out = pl.pallas_call(
        kernel,
        out_shape=jax.ShapeDtypeStruct((2 * per * frames * 4, LANES), F32),
        in_specs=[VMEM] * (4 + groups),
        out_specs=VMEM,
        scratch_shapes=[
            pltpu.VMEM((frames + 2, 2, span, LANES), F32),
            pltpu.VMEM((4, frames * per, 2 * LANES), BF16),
            pltpu.VMEM((4, frames * per, 2 * LANES), BF16),
            pltpu.VMEM((4, frames * per, 2 * LANES), F32),
        ],
        compiler_params=PARAMS,
        name="fine",
    )(taps, jnp.asarray(high), jnp.asarray(low), jnp.asarray(turns), *[in_vmem(piece) for piece in pieces])
    out = out.reshape(2, per, frames // 8, 4, 8, LANES).transpose(0, 1, 2, 4, 3, 5)
    return out.reshape(2, per, frames, 4 * LANES)


def solution(mesh):
    axis = "tm"
    groups = mesh.shape[axis]

    def on_device(signal, coarse_taps, fine_taps):
        pieces = coarse_section(signal, coarse_taps, axis, groups)
        moved = [pieces[0]]
        for step in range(1, groups):
            moved.append(lax.ppermute(pieces[step], axis, [(i, i ^ step) for i in range(groups)]))
        return fine_section(moved, fine_taps, axis, groups)

    return jax.shard_map(
        on_device,
        mesh=mesh,
        in_specs=(P(None, ("streams", "tm")), P(), P()),
        out_specs=P(None, "tm", "streams", None),
        check_vma=False,
    )
```

```python
import math

import jax
import jax.numpy as jnp
import numpy as np
from jax import lax
from jax.experimental import pallas as pl
from jax.experimental.pallas import tpu as pltpu
from jax.sharding import PartitionSpec as P

LANES = 128
F32, BF16 = jnp.float32, jnp.bfloat16


def split_table(table):
    high = np.asarray(table, np.float32).astype(jnp.bfloat16)
    low = (np.asarray(table, np.float64) - high.astype(np.float64)).astype(np.float32).astype(jnp.bfloat16)
    return high, low


def complex_table(turns, points, factor):
    angle = (turns % points) * (2.0 * math.pi / points)
    return np.cos(angle) * factor, -np.sin(angle) * factor


def coarse_table(channels, groups, chunks):
    halves, per = LANES // channels, channels // (groups * chunks)
    k, p = np.arange(channels), np.arange(channels)
    real, imag = complex_table(k[:, None] * p[None, :], channels, 1.0 / math.sqrt(channels))
    table = np.zeros((groups * chunks, 2, halves, per, 2, halves, channels))
    real, imag = real.reshape(-1, per, channels), imag.reshape(-1, per, channels)
    for half in range(halves):
        table[:, 0, half, :, 0, half] = real
        table[:, 0, half, :, 1, half] = -imag
        table[:, 1, half, :, 0, half] = imag
        table[:, 1, half, :, 1, half] = real
    return table.reshape(2 * LANES, 2 * LANES)


def fine_tables(fine):
    radix = fine // LANES
    i = np.arange(LANES)
    real, imag = complex_table(i[:, None] * i[None, :], LANES, 1.0 / math.sqrt(fine))
    table = np.block([[real, imag], [-imag, real]])
    real, imag = complex_table(np.arange(radix)[:, None] * i[None, :], fine, 1.0)
    return table, np.stack([real, imag], axis=1).astype(np.float32)


def split_value(value):
    high = value.astype(BF16)
    return high, (value - high.astype(F32)).astype(BF16)


def dot_nt(left, right):
    return lax.dot_general(left, right, (((1,), (1,)), ((), ())), preferred_element_type=F32)


def dot_nn(left, right):
    return lax.dot_general(left, right, (((1,), (0,)), ((), ())), preferred_element_type=F32)


VMEM = pl.BlockSpec(memory_space=pltpu.VMEM)
ANY = pl.BlockSpec(memory_space=pl.ANY)
PARAMS = pltpu.CompilerParams(vmem_limit_bytes=24 * 1024 * 1024)


def in_vmem(value):
    return pltpu.with_memory_space_constraint(value, pltpu.VMEM)


PAD = 16
PIECES = 4
TAIL = 16


def in_hbm(value):
    return pltpu.with_memory_space_constraint(value, pltpu.HBM)


def pick_rows(table_ref, half, axis, groups, chunks, chunk):
    me = lax.axis_index(axis)
    span = 2 * LANES // (groups * chunks)
    picks = [pl.multiple_of(((me ^ step) * chunks + chunk) * span, span) for step in range(groups)]
    return jnp.concatenate([table_ref[half, pl.ds(pick, span), :] for pick in picks], axis=0)


def send_chunk(axis, groups, chunks, chunk, table_ref, bh_ref, bl_ref, outs):
    span = 2 * LANES // (groups * chunks)
    high = pick_rows(table_ref, 0, axis, groups, chunks, chunk)
    low = pick_rows(table_ref, 1, axis, groups, chunks, chunk)
    both = jnp.concatenate([high, low], axis=0)
    height = high.shape[0]
    for frame in range(2):
        rows = slice(frame * 2 * LANES, (frame + 1) * 2 * LANES)
        first = dot_nt(both, bh_ref[rows])
        result = first[:height] + first[height:] + dot_nt(high, bl_ref[rows])
        for step in range(groups):
            for a in range(2):
                at = (frame * 2 + a) * span
                outs[step][at : at + span] = result[step * span : (step + 1) * span, a * LANES : (a + 1) * LANES]
    bh, bl = bh_ref[4 * LANES :], bl_ref[4 * LANES :]
    tail = dot_nt(bh, high) + dot_nt(bh, low) + dot_nt(bl, high)
    for step in range(groups):
        at = step * span // LANES * LANES
        outs[step][4 * span : 4 * span + 8] = tail[:8, at : at + LANES]


def coarse_kernel(axis, groups, chunks, x_hbm, taps_hbm, table_hbm, *rest):
    outs, (table_ref, bh_ref, bl_ref, taps_ref, xs, ys, bs, sems) = rest[:groups], rest[groups:]
    rows = x_hbm.shape[0]
    taps_count, channels = taps_hbm.shape
    step = rows // PIECES
    loads = [
        pltpu.make_async_copy(x_hbm.at[pl.ds(i * step, step)], xs.at[pl.ds(PAD + i * step, step)], sems.at[i])
        for i in range(PIECES)
    ]
    get_taps = pltpu.make_async_copy(taps_hbm, taps_ref, sems.at[PIECES])
    get_table = pltpu.make_async_copy(table_hbm, table_ref, sems.at[PIECES + 1])
    get_taps.start()
    for load in loads:
        load.start()
    get_table.start()
    zeros = jnp.zeros((PAD, LANES), F32)
    xs[:PAD] = zeros
    xs[PAD + rows :] = zeros
    ys[:PAD] = zeros
    lane = lax.broadcasted_iota(jnp.int32, (1, LANES), 1)
    lower = lane < channels
    get_taps.wait()
    taps = taps_ref[...]
    taps = jnp.concatenate([taps, taps], axis=1)

    def filtered(base, block):
        now = xs[PAD + base : PAD + base + block]
        before = xs[PAD + base - 2 : PAD + base + block - 2]
        ys[PAD + base : PAD + base + block] = pltpu.roll(jnp.where(lower, now, before), channels, 1)
        summed = None
        for parity, source in ((0, xs), (1, ys)):
            for shift in range(taps_count // 4):
                start = PAD + base - 2 * shift - 8
                piece = source[start : start + block + 8]
                near = taps[2 * shift + parity][None, :]
                far = taps[2 * (shift + 4) + parity][None, :]
                term = piece[8:] * near + piece[:block] * far
                summed = term if summed is None else summed + term
        bs[base : base + block] = summed

    def gathered(base, count, at):
        for a in range(2):
            pair = [bs[pl.ds(base + 2 * a + part, count, stride=4), :] for part in range(2)]
            high, low = split_value(jnp.concatenate(pair, axis=1))
            bh_ref[at + a * count : at + (a + 1) * count] = high
            bl_ref[at + a * count : at + (a + 1) * count] = low

    block = 64
    for i, load in enumerate(loads):
        load.wait()
        for base in range(i * step, (i + 1) * step, block):
            filtered(base, block)
        if i % 2:
            gathered(i // 2 * rows // 2, LANES, i // 2 * 2 * LANES)
    filtered(rows, TAIL)
    pairs = [
        jnp.concatenate([bs[pl.ds(rows + 2 * a + part, 4, stride=4), :] for part in range(2)], axis=1)
        for a in range(2)
    ]
    ending = jnp.concatenate(pairs + [jnp.zeros((8, 2 * LANES), F32)], axis=0)
    bh_ref[4 * LANES :], bl_ref[4 * LANES :] = split_value(ending)
    get_table.wait()
    send_chunk(axis, groups, chunks, 0, table_ref, bh_ref, bl_ref, outs)


def coarse_rest_kernel(axis, groups, chunks, chunk, table_ref, bh_ref, bl_ref, *outs):
    send_chunk(axis, groups, chunks, chunk, table_ref, bh_ref, bl_ref, outs)


def coarse_section(signal, coarse_taps, axis, groups, chunks):
    length = signal.shape[1]
    taps_count, channels = coarse_taps.shape
    count = length // LANES
    rows = signal.reshape(2, count, LANES).transpose(1, 0, 2).reshape(2 * count, LANES)
    table = jnp.asarray(np.stack(split_table(coarse_table(channels, groups, chunks))))
    span = 2 * LANES // (groups * chunks)
    height = 4 * LANES + 16
    message = [pltpu.VMEM((4 * span + 8, LANES), F32)] * groups
    first = pl.pallas_call(
        lambda *refs: coarse_kernel(axis, groups, chunks, *refs),
        out_shape=message
        + [pltpu.VMEM((2, 2 * LANES, 2 * LANES), BF16)]
        + [pltpu.VMEM((height, 2 * LANES), BF16)] * 2,
        in_specs=[ANY, ANY, ANY],
        out_specs=[VMEM] * (groups + 3),
        scratch_shapes=[
            pltpu.VMEM((taps_count, channels), F32),
            pltpu.VMEM((2 * count + 2 * PAD, LANES), F32),
            pltpu.VMEM((2 * count + 2 * PAD, LANES), F32),
            pltpu.VMEM((2 * count + PAD, LANES), F32),
            pltpu.SemaphoreType.DMA((PIECES + 2,)),
        ],
        compiler_params=PARAMS,
        cost_estimate=pl.CostEstimate(flops=2000000, bytes_accessed=1000000, transcendentals=0),
        name="coarse",
    )(in_hbm(rows), in_hbm(coarse_taps), in_hbm(table))
    messages, held = [first[:groups]], [in_vmem(value) for value in first[groups:]]
    for chunk in range(1, chunks):
        more = pl.pallas_call(
            lambda *refs: coarse_rest_kernel(axis, groups, chunks, chunk, *refs),
            out_shape=message,
            in_specs=[VMEM] * 3,
            out_specs=[VMEM] * groups,
            compiler_params=PARAMS,
            cost_estimate=pl.CostEstimate(flops=2000000, bytes_accessed=1000000, transcendentals=0),
            name="coarse_rest",
        )(*held)
        messages.append(more)
    return messages


def fine_kernel(axis, groups, chunks, chunk, *refs):
    taps_ref, high_ref, low_ref, turn_ref = refs[:4]
    pieces = refs[4 : 4 + groups]
    out_hbm, xs, yh, yl, zs, os, sem = refs[-7:]
    span = 2 * LANES // (groups * chunks)
    per = span // 4
    frames = 2 * groups
    taps_count = taps_ref.shape[1]
    me = lax.axis_index(axis)
    for step in range(groups):
        owner = me ^ step
        for frame in range(2):
            for a in range(2):
                at = (frame * 2 + a) * span
                xs[2 * owner + frame, a] = pieces[step][at : at + span]
    for step in range(groups):
        owner = me ^ step
        tail = jnp.transpose(pieces[step][4 * span : 4 * span + 8])
        at = step * span % LANES
        tail = tail[at : at + span]
        for a in range(2):
            into = xs[2 * owner + 2, a, :, 0:4]
            xs[2 * owner + 2, a, :, 0:4] = into + tail[:, 4 * a : 4 * a + 4]
    height = frames * per
    for a in range(2):
        for h in range(2):
            phase = 2 * a + h
            taps = [taps_ref[phase, j : j + 1] for j in range(min(frames, taps_count))]
            sums = []
            for part in range(2):
                at = (2 * part + h) * per
                x = [xs[m, a, at : at + per] for m in range(frames)]
                sums.append([sum((x[m - j] * taps[j] for j in range(1, min(m + 1, taps_count))), x[m] * taps[0]) for m in range(frames)])
            if per % 8 == 0:
                joined = [jnp.concatenate(values, axis=0) for values in sums]
                high, low = split_value(jnp.concatenate(joined, axis=1))
                yh[phase * height : (phase + 1) * height] = high
                yl[phase * height : (phase + 1) * height] = low
            else:
                for part in range(2):
                    for m in range(frames):
                        high, low = split_value(sums[part][m])
                        at = phase * height + m * per
                        yh[at : at + per, part * LANES : (part + 1) * LANES] = high
                        yl[at : at + per, part * LANES : (part + 1) * LANES] = low
    high, low = high_ref[...], low_ref[...]
    zs[...] = dot_nn(yh[...], high) + dot_nn(yl[...], high) + dot_nn(yh[...], low)
    size = min(8, per)
    blocks = frames // 8
    for at in range(0, height, 8):
        z = []
        for phase in range(4):
            row = phase * height + at
            real, imag = zs[row : row + 8, :LANES], zs[row : row + 8, LANES:]
            if phase:
                c, s = turn_ref[phase, 0:1], turn_ref[phase, 1:2]
                real, imag = real * c - imag * s, real * s + imag * c
            z.append((real, imag))
        (ar, ai), (br, bi), (cr, ci), (dr, di) = z
        pr, pi, qr, qi = ar + cr, ai + ci, ar - cr, ai - ci
        ur, ui, vr, vi = br + dr, bi + di, br - dr, bi - di
        reals = (pr + ur, qr + vi, pr - ur, qr - vi)
        imags = (pi + ui, qi - vr, pi - ui, qi + vr)
        for part, values in enumerate((reals, imags)):
            for r, value in enumerate(values):
                for inner in range(0, 8, size):
                    m, k = divmod(at + inner, per)
                    row = ((k * blocks + m // 8) * 4 + r) * 8 + m % 8
                    os[part, pl.ds(row, size, stride=32 * blocks), :] = value[inner : inner + size]
    length = per * blocks * 32
    copies = [
        pltpu.make_async_copy(os.at[part], out_hbm.at[part, pl.ds(chunk * length, length)], sem.at[part])
        for part in range(2)
    ]
    for copy in copies:
        copy.start()
    for copy in copies:
        copy.wait()


def fine_section(moved, fine_taps, axis, groups, chunks):
    taps_count, fine = fine_taps.shape
    span = 2 * LANES // (groups * chunks)
    per, frames = span // 4, 2 * groups
    taps = fine_taps.reshape(taps_count, LANES, fine // LANES).transpose(2, 0, 1)
    table, turns = fine_tables(fine)
    high, low = split_table(table)
    shared = [taps, jnp.asarray(high), jnp.asarray(low), jnp.asarray(turns)]
    height = 4 * frames * per
    length = per * frames * 4
    out = None
    for chunk in range(chunks):
        more = [] if out is None else [out]
        out = pl.pallas_call(
            lambda *refs: fine_kernel(axis, groups, chunks, chunk, *refs),
            out_shape=pltpu.HBM((2, chunks * length, LANES), F32),
            in_specs=[VMEM] * (4 + groups) + [ANY] * len(more),
            out_specs=ANY,
            scratch_shapes=[
                pltpu.VMEM((frames + 2, 2, span, LANES), F32),
                pltpu.VMEM((height, 2 * LANES), BF16),
                pltpu.VMEM((height, 2 * LANES), BF16),
                pltpu.VMEM((height, 2 * LANES), F32),
                pltpu.VMEM((2, length, LANES), F32),
                pltpu.SemaphoreType.DMA((2,)),
            ],
            input_output_aliases={4 + groups: 0} if more else {},
            compiler_params=PARAMS,
            cost_estimate=pl.CostEstimate(flops=2000000, bytes_accessed=1000000, transcendentals=0),
            name="fine",
        )(*[in_vmem(value) for value in shared + list(moved[chunk])], *more)
    out = out.reshape(2, chunks * per, frames // 8, 4, 8, LANES).transpose(0, 1, 2, 4, 3, 5)
    return out.reshape(2, chunks * per, frames, 4 * LANES)


def solution(mesh):
    axis = "tm"
    groups = mesh.shape[axis]

    def on_device(signal, coarse_taps, fine_taps):
        chunks = max(1, coarse_taps.shape[1] // (groups * 8))
        messages = coarse_section(signal, coarse_taps, axis, groups, chunks)
        moved = []
        for message in messages:
            arrived = {0: message[0]}
            for step in range(groups - 1, 0, -1):
                arrived[step] = lax.ppermute(message[step], axis, [(i, i ^ step) for i in range(groups)])
            moved.append([arrived[step] for step in range(groups)])
        return fine_section(moved, fine_taps, axis, groups, chunks)

    return jax.shard_map(
        on_device,
        mesh=mesh,
        in_specs=(P(None, ("streams", "tm")), P(), P()),
        out_specs=P(None, "tm", "streams", None),
        check_vma=False,
    )
```

```python
import math

import jax
import jax.numpy as jnp
import numpy as np
from jax import lax
from jax.experimental import pallas as pl
from jax.experimental.pallas import tpu as pltpu
from jax.sharding import PartitionSpec as P

LANES = 128
F32, BF16 = jnp.float32, jnp.bfloat16


def split_table(table):
    high = np.asarray(table, np.float32).astype(jnp.bfloat16)
    low = (np.asarray(table, np.float64) - high.astype(np.float64)).astype(np.float32).astype(jnp.bfloat16)
    return high, low


def complex_table(turns, points, factor):
    angle = (turns % points) * (2.0 * math.pi / points)
    return np.cos(angle) * factor, -np.sin(angle) * factor


def coarse_table(channels, groups):
    halves, per = LANES // channels, channels // groups
    k, p = np.arange(channels), np.arange(channels)
    real, imag = complex_table(k[:, None] * p[None, :], channels, 1.0 / math.sqrt(channels))
    table = np.zeros((groups, 2, halves, per, 2, halves, channels))
    real, imag = real.reshape(-1, per, channels), imag.reshape(-1, per, channels)
    for half in range(halves):
        table[:, 0, half, :, 0, half] = real
        table[:, 0, half, :, 1, half] = -imag
        table[:, 1, half, :, 0, half] = imag
        table[:, 1, half, :, 1, half] = real
    return table.reshape(2 * LANES, 2 * LANES)


def fine_tables(fine):
    radix = fine // LANES
    i = np.arange(LANES)
    real, imag = complex_table(i[:, None] * i[None, :], LANES, 1.0 / math.sqrt(fine))
    table = np.block([[real, imag], [-imag, real]])
    real, imag = complex_table(np.arange(radix)[:, None] * i[None, :], fine, 1.0)
    return table, np.stack([real, imag], axis=1).astype(np.float32)


def split_value(value):
    high = value.astype(BF16)
    return high, (value - high.astype(F32)).astype(BF16)


def dot_nt(left, right):
    return lax.dot_general(left, right, (((1,), (1,)), ((), ())), preferred_element_type=F32)


def dot_nn(left, right):
    return lax.dot_general(left, right, (((1,), (0,)), ((), ())), preferred_element_type=F32)


VMEM = pl.BlockSpec(memory_space=pltpu.VMEM)
ANY = pl.BlockSpec(memory_space=pl.ANY)
PARAMS = pltpu.CompilerParams(vmem_limit_bytes=24 * 1024 * 1024)


def in_vmem(value):
    return pltpu.with_memory_space_constraint(value, pltpu.VMEM)


PAD = 16
PIECES = 4
COST = pl.CostEstimate(flops=2000000, bytes_accessed=1000000, transcendentals=0)


def in_hbm(value):
    return pltpu.with_memory_space_constraint(value, pltpu.HBM)


def pick_rows(table_ref, half, axis, groups):
    me = lax.axis_index(axis)
    span = 2 * LANES // groups
    picks = [pl.multiple_of((me ^ step) * span, span) for step in range(groups)]
    return jnp.concatenate([table_ref[half, pl.ds(pick, span), :] for pick in picks], axis=0)


def filter_rows(xs, ys, bs, taps, base, block, origin):
    channels = LANES // 2
    lower = lax.broadcasted_iota(jnp.int32, (1, LANES), 1) < channels
    now = xs[PAD + base : PAD + base + block]
    before = xs[PAD + base - 2 : PAD + base + block - 2]
    at = base - origin
    ys[PAD + at : PAD + at + block] = pltpu.roll(jnp.where(lower, now, before), channels, 1)
    if bs is None:
        return
    summed = None
    for parity, source, start in ((0, xs, PAD + base), (1, ys, PAD + at)):
        for shift in range(taps.shape[0] // 4):
            low = start - 2 * shift - 8
            piece = source[low : low + block + 8]
            near = taps[2 * shift + parity][None, :]
            far = taps[2 * (shift + 4) + parity][None, :]
            term = piece[8:] * near + piece[:block] * far
            summed = term if summed is None else summed + term
    bs[at : at + block] = summed


def gather_rows(bs, base, count):
    parts = [
        jnp.concatenate([bs[pl.ds(base + 2 * a + part, count, stride=4), :] for part in range(2)], axis=1)
        for a in range(2)
    ]
    return jnp.concatenate(parts, axis=0)


def send_frame(groups, high, low, gathered, outs):
    span = 2 * LANES // groups
    bh, bl = split_value(gathered)
    result = dot_nt(high, bh) + dot_nt(low, bh) + dot_nt(high, bl)
    for step in range(groups):
        for a in range(2):
            outs[step][a * span : (a + 1) * span] = result[step * span : (step + 1) * span, a * LANES : (a + 1) * LANES]


def coarse_kernel(axis, groups, x_hbm, taps_hbm, table_hbm, *rest):
    outs, (table_ref, taps_out, xs, taps_ref, ys, bs, yt, bt, sems) = rest[:groups], rest[groups:]
    rows = x_hbm.shape[0]
    span = 2 * LANES // groups
    step = rows // PIECES
    loads = [
        pltpu.make_async_copy(x_hbm.at[pl.ds(i * step, step)], xs.at[pl.ds(PAD + i * step, step)], sems.at[i])
        for i in range(PIECES)
    ]
    get_taps = pltpu.make_async_copy(taps_hbm, taps_ref, sems.at[PIECES])
    get_table = pltpu.make_async_copy(table_hbm, table_ref, sems.at[PIECES + 1])
    get_taps.start()
    for load in loads[: PIECES // 2]:
        load.start()
    get_table.start()
    for load in loads[PIECES // 2 :]:
        load.start()
    zeros = jnp.zeros((PAD, LANES), F32)
    xs[:PAD] = zeros
    xs[PAD + rows :] = zeros
    ys[:PAD] = zeros
    get_taps.wait()
    taps = taps_ref[...]
    taps = jnp.concatenate([taps, taps], axis=1)
    taps_out[...] = taps
    block = 64
    for i in range(PIECES // 2):
        loads[i].wait()
        for base in range(i * step, (i + 1) * step, block):
            filter_rows(xs, ys, bs, taps, base, block, 0)
    for load in loads[PIECES // 2 :]:
        load.wait()
    get_table.wait()
    high, low = pick_rows(table_ref, 0, axis, groups), pick_rows(table_ref, 1, axis, groups)
    send_frame(groups, high, low, gather_rows(bs, 0, LANES), outs)
    yt[:PAD] = zeros
    filter_rows(xs, yt, None, taps, rows - 16, 16, rows - 16)
    filter_rows(xs, yt, bt, taps, rows, 16, rows - 16)
    th, tl = split_value(gather_rows(bt, 16, 4))
    tail = dot_nt(th, high) + dot_nt(th, low) + dot_nt(tl, high)
    for step in range(groups):
        at = step * span // LANES * LANES
        outs[step][2 * span : 2 * span + 8] = tail[:, at : at + LANES]


def coarse_rest_kernel(axis, groups, table_ref, taps_ref, xs, *rest):
    outs, (ys, bs) = rest[:groups], rest[groups:]
    rows = xs.shape[0] - 2 * PAD
    taps = taps_ref[...]
    block = 64
    origin = rows // 2 - 16
    filter_rows(xs, ys, None, taps, origin, 16, origin)
    for base in range(rows // 2, rows, block):
        filter_rows(xs, ys, bs, taps, base, block, origin)
    high, low = pick_rows(table_ref, 0, axis, groups), pick_rows(table_ref, 1, axis, groups)
    send_frame(groups, high, low, gather_rows(bs, 16, LANES), outs)


def coarse_section(signal, coarse_taps, axis, groups):
    length = signal.shape[1]
    taps_count, channels = coarse_taps.shape
    count = length // LANES
    rows = signal.reshape(2, count, LANES).transpose(1, 0, 2).reshape(2 * count, LANES)
    table = jnp.asarray(np.stack(split_table(coarse_table(channels, groups))))
    span = 2 * LANES // groups
    first = pl.pallas_call(
        lambda *refs: coarse_kernel(axis, groups, *refs),
        out_shape=[pltpu.VMEM((2 * span + 8, LANES), F32)] * groups
        + [
            pltpu.VMEM((2, 2 * LANES, 2 * LANES), BF16),
            pltpu.VMEM((taps_count, LANES), F32),
            pltpu.VMEM((2 * count + 2 * PAD, LANES), F32),
        ],
        in_specs=[ANY] * 3,
        out_specs=[VMEM] * (groups + 3),
        scratch_shapes=[
            pltpu.VMEM((taps_count, channels), F32),
            pltpu.VMEM((count + PAD, LANES), F32),
            pltpu.VMEM((count, LANES), F32),
            pltpu.VMEM((PAD + 32, LANES), F32),
            pltpu.VMEM((32, LANES), F32),
            pltpu.SemaphoreType.DMA((PIECES + 2,)),
        ],
        compiler_params=PARAMS,
        cost_estimate=COST,
        name="coarse",
    )(in_hbm(rows), in_hbm(coarse_taps), in_hbm(table))
    second = pl.pallas_call(
        lambda *refs: coarse_rest_kernel(axis, groups, *refs),
        out_shape=[pltpu.VMEM((2 * span, LANES), F32)] * groups,
        in_specs=[VMEM] * 3,
        out_specs=[VMEM] * groups,
        scratch_shapes=[
            pltpu.VMEM((count + 16 + PAD, LANES), F32),
            pltpu.VMEM((count + 16, LANES), F32),
        ],
        compiler_params=PARAMS,
        cost_estimate=COST,
        name="coarse_rest",
    )(*[in_vmem(value) for value in first[groups:]])
    return first[:groups], second


def place(axis, groups, pieces, xs):
    span = 2 * LANES // groups
    me = lax.axis_index(axis)
    for step in range(groups):
        for a in range(2):
            xs[me ^ step, a] = pieces[step][a * span : (a + 1) * span]


def terms(xs, taps, parity, m, a, rows):
    taps_count = len(taps)
    return [xs[g, a, rows] * taps[m - 2 * g - parity] for g in range((m - parity) // 2, -1, -1) if m - 2 * g - parity < taps_count] if m >= parity else []


def fine_start_kernel(axis, groups, taps_ref, *refs):
    pieces, (out_ref, xs) = refs[:groups], refs[groups:]
    span = 2 * LANES // groups
    per, frames = span // 4, 2 * groups
    me = lax.axis_index(axis)
    place(axis, groups, pieces, xs)
    for step in range(groups):
        tail = jnp.transpose(pieces[step][2 * span : 2 * span + 8])
        at = step * span % LANES
        tail = tail[at : at + span]
        owner = (me ^ step) + 1
        for a in range(2):
            xs[owner, a, :, 0:4] = xs[owner, a, :, 0:4] + tail[:, 4 * a : 4 * a + 4]
    taps_count = taps_ref.shape[1]
    for a in range(2):
        for h in range(2):
            phase = 2 * a + h
            taps = [taps_ref[phase, j : j + 1] for j in range(taps_count)]
            for part in range(2):
                rows = slice((2 * part + h) * per, (2 * part + h + 1) * per)
                for m in range(frames):
                    out_ref[phase, part, m * per : (m + 1) * per] = sum(terms(xs, taps, 0, m, a, rows))


def fine_kernel(axis, groups, taps_ref, high_ref, low_ref, turn_ref, acc_ref, *refs):
    pieces, (out_hbm, xs, fs, yh, yl, zs, os, sem) = refs[:groups], refs[groups:]
    span = 2 * LANES // groups
    per, frames = span // 4, 2 * groups
    taps_count = taps_ref.shape[1]
    place(axis, groups, pieces, xs)
    for a in range(2):
        for h in range(2):
            phase = 2 * a + h
            taps = [taps_ref[phase, j : j + 1] for j in range(taps_count)]
            for part in range(2):
                rows = slice((2 * part + h) * per, (2 * part + h + 1) * per)
                for m in range(frames):
                    at = m * per
                    fs[phase, part, at : at + per] = sum(terms(xs, taps, 1, m, a, rows), acc_ref[phase, part, at : at + per])
    high, low = high_ref[...], low_ref[...]
    blocks = frames // 8
    share = per // SHARES
    height = share * frames
    copies = []
    for turn in range(SHARES):
        for phase in range(4):
            columns = []
            for part in range(2):
                picked = [fs[phase, part, pl.ds(turn * share + k, frames, stride=per), :] for k in range(share)]
                columns.append(jnp.concatenate(picked, axis=0))
            first, second = split_value(jnp.concatenate(columns, axis=1))
            yh[turn, phase * height : (phase + 1) * height] = first
            yl[turn, phase * height : (phase + 1) * height] = second
        zs[turn] = dot_nn(yh[turn], high) + dot_nn(yl[turn], high) + dot_nn(yh[turn], low)
        for at in range(0, height, 8):
            z = []
            for phase in range(4):
                row = phase * height + at
                real, imag = zs[turn, row : row + 8, :LANES], zs[turn, row : row + 8, LANES:]
                if phase:
                    c, s = turn_ref[phase, 0:1], turn_ref[phase, 1:2]
                    real, imag = real * c - imag * s, real * s + imag * c
                z.append((real, imag))
            (ar, ai), (br, bi), (cr, ci), (dr, di) = z
            pr, pi, qr, qi = ar + cr, ai + ci, ar - cr, ai - ci
            ur, ui, vr, vi = br + dr, bi + di, br - dr, bi - di
            reals = (pr + ur, qr + vi, pr - ur, qr - vi)
            imags = (pi + ui, qi - vr, pi - ui, qi + vr)
            for part, values in enumerate((reals, imags)):
                for r, value in enumerate(values):
                    row = ((turn * share * blocks + at // 8) * 4 + r) * 8
                    os[part, row : row + 8, :] = value
        length = share * blocks * 32
        for part in range(2):
            place_of = pl.ds(turn * length, length)
            copy = pltpu.make_async_copy(os.at[part, place_of], out_hbm.at[part, place_of], sem.at[2 * turn + part])
            copy.start()
            copies.append(copy)
    for copy in copies:
        copy.wait()


SHARES = 2


def fine_section(moved, fine_taps, axis, groups):
    taps_count, fine = fine_taps.shape
    span = 2 * LANES // groups
    per, frames = span // 4, 2 * groups
    taps = in_vmem(fine_taps.reshape(taps_count, LANES, fine // LANES).transpose(2, 0, 1))
    table, turns = fine_tables(fine)
    high, low = split_table(table)
    started = pl.pallas_call(
        lambda *refs: fine_start_kernel(axis, groups, *refs),
        out_shape=pltpu.VMEM((4, 2, frames * per, LANES), F32),
        in_specs=[VMEM] * (1 + groups),
        out_specs=VMEM,
        scratch_shapes=[pltpu.VMEM((groups + 1, 2, span, LANES), F32)],
        compiler_params=PARAMS,
        cost_estimate=COST,
        name="fine_start",
    )(taps, *[in_vmem(value) for value in moved[0]])
    height = 4 * frames * per // SHARES
    length = per * frames * 4
    shared = [jnp.asarray(high), jnp.asarray(low), jnp.asarray(turns), started]
    out = pl.pallas_call(
        lambda *refs: fine_kernel(axis, groups, *refs),
        out_shape=pltpu.HBM((2, length, LANES), F32),
        in_specs=[VMEM] * (5 + groups),
        out_specs=ANY,
        scratch_shapes=[
            pltpu.VMEM((groups + 1, 2, span, LANES), F32),
            pltpu.VMEM((4, 2, frames * per, LANES), F32),
            pltpu.VMEM((SHARES, height, 2 * LANES), BF16),
            pltpu.VMEM((SHARES, height, 2 * LANES), BF16),
            pltpu.VMEM((SHARES, height, 2 * LANES), F32),
            pltpu.VMEM((2, length, LANES), F32),
            pltpu.SemaphoreType.DMA((2 * SHARES,)),
        ],
        compiler_params=PARAMS,
        cost_estimate=COST,
        name="fine",
    )(taps, *[in_vmem(value) for value in shared + list(moved[1])])
    out = out.reshape(2, per, frames // 8, 4, 8, LANES).transpose(0, 1, 2, 4, 3, 5)
    return out.reshape(2, per, frames, 4 * LANES)


def solution(mesh):
    axis = "tm"
    groups = mesh.shape[axis]

    def on_device(signal, coarse_taps, fine_taps):
        moved = []
        for message in coarse_section(signal, coarse_taps, axis, groups):
            arrived = [message[0]]
            for step in range(1, groups):
                arrived.append(lax.ppermute(message[step], axis, [(i, i ^ step) for i in range(groups)]))
            moved.append(arrived)
        return fine_section(moved, fine_taps, axis, groups)

    return jax.shard_map(
        on_device,
        mesh=mesh,
        in_specs=(P(None, ("streams", "tm")), P(), P()),
        out_specs=P(None, "tm", "streams", None),
        check_vma=False,
    )
```

```python
import math

import jax
import jax.numpy as jnp
import numpy as np
from jax import lax
from jax.experimental import pallas as pl
from jax.experimental.pallas import tpu as pltpu
from jax.sharding import PartitionSpec as P

LANES = 128
F32, BF16 = jnp.float32, jnp.bfloat16


def split_table(table):
    high = np.asarray(table, np.float32).astype(jnp.bfloat16)
    low = (np.asarray(table, np.float64) - high.astype(np.float64)).astype(np.float32).astype(jnp.bfloat16)
    return high, low


def complex_table(turns, points, factor):
    angle = (turns % points) * (2.0 * math.pi / points)
    return np.cos(angle) * factor, -np.sin(angle) * factor


def coarse_table(channels, groups, shares):
    halves, per = LANES // channels, channels // (groups * shares)
    k, p = np.arange(channels), np.arange(channels)
    real, imag = complex_table(k[:, None] * p[None, :], channels, 1.0 / math.sqrt(channels))
    table = np.zeros((groups * shares, 2, halves, per, 2, halves, channels))
    real, imag = real.reshape(-1, per, channels), imag.reshape(-1, per, channels)
    for half in range(halves):
        table[:, 0, half, :, 0, half] = real
        table[:, 0, half, :, 1, half] = -imag
        table[:, 1, half, :, 0, half] = imag
        table[:, 1, half, :, 1, half] = real
    return table.reshape(2 * LANES, 2 * LANES)


def fine_tables(fine):
    radix = fine // LANES
    i = np.arange(LANES)
    real, imag = complex_table(i[:, None] * i[None, :], LANES, 1.0 / math.sqrt(fine))
    table = np.block([[real, imag], [-imag, real]])
    real, imag = complex_table(np.arange(radix)[:, None] * i[None, :], fine, 1.0)
    return table, np.stack([real, imag], axis=1).astype(np.float32)


def split_value(value):
    high = value.astype(BF16)
    return high, (value - high.astype(F32)).astype(BF16)


def dot_nt(left, right):
    return lax.dot_general(left, right, (((1,), (1,)), ((), ())), preferred_element_type=F32)


def dot_nn(left, right):
    return lax.dot_general(left, right, (((1,), (0,)), ((), ())), preferred_element_type=F32)


VMEM = pl.BlockSpec(memory_space=pltpu.VMEM)
ANY = pl.BlockSpec(memory_space=pl.ANY)
PARAMS = pltpu.CompilerParams(vmem_limit_bytes=24 * 1024 * 1024)


def in_vmem(value):
    return pltpu.with_memory_space_constraint(value, pltpu.VMEM)


PAD = 16
PIECES = 4
COST = pl.CostEstimate(flops=2000000, bytes_accessed=1000000, transcendentals=0)


def in_hbm(value):
    return pltpu.with_memory_space_constraint(value, pltpu.HBM)


def pick_rows(table_ref, half, axis, groups):
    me = lax.axis_index(axis)
    span = 2 * LANES // groups
    picks = [pl.multiple_of((me ^ step) * span, span) for step in range(groups)]
    return jnp.concatenate([table_ref[half, pl.ds(pick, span), :] for pick in picks], axis=0)


def filter_rows(xs, ys, bs, taps, base, block, origin):
    channels = LANES // 2
    lower = lax.broadcasted_iota(jnp.int32, (1, LANES), 1) < channels
    now = xs[PAD + base : PAD + base + block]
    before = xs[PAD + base - 2 : PAD + base + block - 2]
    at = base - origin
    ys[PAD + at : PAD + at + block] = pltpu.roll(jnp.where(lower, now, before), channels, 1)
    if bs is None:
        return
    summed = None
    for parity, source, start in ((0, xs, PAD + base), (1, ys, PAD + at)):
        for shift in range(taps.shape[0] // 4):
            low = start - 2 * shift - 8
            piece = source[low : low + block + 8]
            near = taps[2 * shift + parity][None, :]
            far = taps[2 * (shift + 4) + parity][None, :]
            term = piece[8:] * near + piece[:block] * far
            summed = term if summed is None else summed + term
    bs[at : at + block] = summed


def gather_rows(bs, base, count):
    parts = [
        jnp.concatenate([bs[pl.ds(base + 2 * a + part, count, stride=4), :] for part in range(2)], axis=1)
        for a in range(2)
    ]
    return jnp.concatenate(parts, axis=0)


def frame_blocks(groups, high, low, gathered):
    span = 2 * LANES // groups
    bh, bl = split_value(gathered)
    result = dot_nt(high, bh) + dot_nt(low, bh) + dot_nt(high, bl)
    return [
        [result[step * span : (step + 1) * span, a * LANES : (a + 1) * LANES] for a in range(2)]
        for step in range(groups)
    ]


def coarse_kernel(axis, groups, x_hbm, taps_hbm, table_hbm, *rest):
    lots = 1 + groups // 2
    outs, (table_ref, taps_out, xs, taps_ref, ys, bs, yt, bt, sems) = rest[:lots], rest[lots:]
    rows = x_hbm.shape[0]
    span = 2 * LANES // groups
    step = rows // PIECES
    loads = [
        pltpu.make_async_copy(x_hbm.at[pl.ds(i * step, step)], xs.at[pl.ds(PAD + i * step, step)], sems.at[i])
        for i in range(PIECES)
    ]
    get_taps = pltpu.make_async_copy(taps_hbm, taps_ref, sems.at[PIECES])
    get_table = pltpu.make_async_copy(table_hbm, table_ref, sems.at[PIECES + 1])
    get_taps.start()
    for load in loads[: PIECES // 2]:
        load.start()
    get_table.start()
    for load in loads[PIECES // 2 :]:
        load.start()
    zeros = jnp.zeros((PAD, LANES), F32)
    xs[:PAD] = zeros
    xs[PAD + rows :] = zeros
    ys[:PAD] = zeros
    get_taps.wait()
    taps = taps_ref[...]
    taps = jnp.concatenate([taps, taps], axis=1)
    taps_out[...] = taps
    block = 64
    for i in range(PIECES // 2):
        loads[i].wait()
        for base in range(i * step, (i + 1) * step, block):
            filter_rows(xs, ys, bs, taps, base, block, 0)
    for load in loads[PIECES // 2 :]:
        load.wait()
    get_table.wait()
    high, low = pick_rows(table_ref, 0, axis, groups), pick_rows(table_ref, 1, axis, groups)
    slots = [(outs[0], 0)] + [(outs[1 + s // 2], s % 2 * 2 * span if s > 1 else 0) for s in range(1, groups)]
    for (out, at), block in zip(slots, frame_blocks(groups, high, low, gather_rows(bs, 0, LANES))):
        for a in range(2):
            out[at + a * span : at + (a + 1) * span] = block[a]
    yt[:PAD] = zeros
    filter_rows(xs, yt, None, taps, rows - 16, 16, rows - 16)
    filter_rows(xs, yt, bt, taps, rows, 16, rows - 16)
    th, tl = split_value(gather_rows(bt, 16, 4))
    tail = dot_nt(th, high) + dot_nt(th, low) + dot_nt(tl, high)
    for step in [0, 1, *range(2, groups, 2)]:
        out, lanes = slots[step][0], step * span // LANES * LANES
        out[out.shape[0] - 8 :] = tail[:, lanes : lanes + LANES]


def coarse_rest_kernel(axis, groups, shares, table_ref, taps_ref, xs, *rest):
    lots = 2 + shares * (groups - 2)
    outs, (ys, bs) = rest[:lots], rest[lots:]
    small = 2 * LANES // (groups * shares)
    rows = xs.shape[0] - 2 * PAD
    taps = taps_ref[...]
    block = 64
    origin = rows // 2 - 16
    filter_rows(xs, ys, None, taps, origin, 16, origin)
    for base in range(rows // 2, rows, block):
        filter_rows(xs, ys, bs, taps, base, block, origin)
    high, low = pick_rows(table_ref, 0, axis, groups), pick_rows(table_ref, 1, axis, groups)
    for step, block in enumerate(frame_blocks(groups, high, low, gather_rows(bs, 16, LANES))):
        for share in range(shares):
            out, at = (outs[step], share * 2 * small) if step < 2 else (outs[share * (groups - 2) + step], 0)
            for a in range(2):
                out[at + a * small : at + (a + 1) * small] = block[a][share * small : (share + 1) * small]


def coarse_section(signal, coarse_taps, axis, groups, shares):
    length = signal.shape[1]
    taps_count, channels = coarse_taps.shape
    count = length // LANES
    rows = signal.reshape(2, count, LANES).transpose(1, 0, 2).reshape(2 * count, LANES)
    table = jnp.asarray(np.stack(split_table(coarse_table(channels, groups, shares))))
    span = 2 * LANES // groups
    lots = 1 + groups // 2
    first = pl.pallas_call(
        lambda *refs: coarse_kernel(axis, groups, *refs),
        out_shape=[pltpu.VMEM((2 * span + 8, LANES), F32)] * 2
        + [pltpu.VMEM((4 * span + 8, LANES), F32)] * (groups // 2 - 1)
        + [
            pltpu.VMEM((2, 2 * LANES, 2 * LANES), BF16),
            pltpu.VMEM((taps_count, LANES), F32),
            pltpu.VMEM((2 * count + 2 * PAD, LANES), F32),
        ],
        in_specs=[ANY] * 3,
        out_specs=[VMEM] * (lots + 3),
        scratch_shapes=[
            pltpu.VMEM((taps_count, channels), F32),
            pltpu.VMEM((count + PAD, LANES), F32),
            pltpu.VMEM((count, LANES), F32),
            pltpu.VMEM((PAD + 32, LANES), F32),
            pltpu.VMEM((32, LANES), F32),
            pltpu.SemaphoreType.DMA((PIECES + 2,)),
        ],
        compiler_params=PARAMS,
        cost_estimate=COST,
        name="coarse",
    )(in_hbm(rows), in_hbm(coarse_taps), in_hbm(table))
    second = pl.pallas_call(
        lambda *refs: coarse_rest_kernel(axis, groups, shares, *refs),
        out_shape=[pltpu.VMEM((2 * span, LANES), F32)] * 2
        + [pltpu.VMEM((2 * span // shares, LANES), F32)] * (shares * (groups - 2)),
        in_specs=[VMEM] * 3,
        out_specs=[VMEM] * (2 + shares * (groups - 2)),
        scratch_shapes=[
            pltpu.VMEM((count + 16 + PAD, LANES), F32),
            pltpu.VMEM((count + 16, LANES), F32),
        ],
        compiler_params=PARAMS,
        cost_estimate=COST,
        name="coarse_rest",
    )(*[in_vmem(value) for value in first[lots:]])
    return first[:lots], second


def terms(xs, taps, parity, m, a, rows):
    reach = [(g, m - 2 * g - parity) for g in range((m - parity) // 2, -1, -1)]
    height = rows.stop - rows.start
    return [xs[g, a, rows] * tiled(taps[j], height) for g, j in reach if j < len(taps)]


def tiled(tap, height):
    return tap[:height] if height <= 8 else jnp.concatenate([tap] * (height // 8), axis=0)


def fine_start_kernel(axis, groups, shares, taps_ref, *refs):
    pieces, (out_ref, xs) = refs[:groups], refs[groups:]
    span = 2 * LANES // groups
    small, per, frames = span // shares, span // (4 * shares), 2 * groups
    me = lax.axis_index(axis)
    for step in range(groups):
        for a in range(2):
            xs[me ^ step, a] = pieces[step][a * span : (a + 1) * span]
    for step in range(groups):
        tail = jnp.transpose(pieces[step][pieces[step].shape[0] - 8 :])
        at = step * span % LANES
        tail = tail[at : at + span]
        owner = (me ^ step) + 1
        for a in range(2):
            xs[owner, a, :, 0:4] = xs[owner, a, :, 0:4] + tail[:, 4 * a : 4 * a + 4]
    for a in range(2):
        for h in range(2):
            phase = 2 * a + h
            taps = [taps_ref[phase, j] for j in range(taps_ref.shape[1])]
            for share in range(shares):
                for part in range(2):
                    at = share * small + (2 * part + h) * per
                    for m in range(frames):
                        value = sum(terms(xs, taps, 0, m, a, slice(at, at + per)))
                        out_ref[share, phase, part, m * per : (m + 1) * per] = value


def fine_kernel(axis, groups, shares, share, taps_ref, table_ref, turn_ref, acc_ref, *refs):
    pieces, (out_hbm, xs, fs, yh, yl, zs, os, sem) = refs[:groups], refs[-8:]
    small = 2 * LANES // (groups * shares)
    per, frames = small // 4, 2 * groups
    me = lax.axis_index(axis)
    for step in range(groups):
        base = share * 2 * small if step < 2 else 0
        for a in range(2):
            xs[me ^ step, a] = pieces[step][base + a * small : base + (a + 1) * small]
    turns = 2 if per >= 16 else 1
    part_of = per // turns
    height = part_of * frames
    length = height * 4
    high, low = table_ref[0], table_ref[1]
    copies = [
        pltpu.make_async_copy(
            os.at[part, pl.ds(turn * length, length)],
            out_hbm.at[part, pl.ds((share * turns + turn) * length, length)],
            sem.at[2 * turn + part],
        )
        for turn in range(turns)
        for part in range(2)
    ]

    def run(turn):
        top = turn * 4 * height
        for a in range(2):
            for h in range(2):
                phase = 2 * a + h
                taps = [taps_ref[phase, j] for j in range(taps_ref.shape[1])]
                columns = []
                for part in range(2):
                    at = (2 * part + h) * per + turn * part_of
                    rows = slice(at, at + part_of)
                    for m in range(frames):
                        at = m * per + turn * part_of
                        value = sum(terms(xs, taps, 1, m, a, rows), acc_ref[share, phase, part, at : at + part_of])
                        at = m * part_of
                        fs[turn, phase, part, at : at + part_of] = value
                    picked = [fs[turn, phase, part, pl.ds(k, frames, stride=part_of), :] for k in range(part_of)]
                    columns.append(jnp.concatenate(picked, axis=0))
                first, second = split_value(jnp.concatenate(columns, axis=1))
                at = top + phase * height
                yh[at : at + height] = first
                yl[at : at + height] = second
        left, right = yh[top : top + 4 * height], yl[top : top + 4 * height]
        zs[top : top + 4 * height] = dot_nn(left, high) + dot_nn(right, high) + dot_nn(left, low)
        for at in range(0, height, 8):
            z = []
            for phase in range(4):
                row = top + phase * height + at
                real, imag = zs[row : row + 8, :LANES], zs[row : row + 8, LANES:]
                if phase:
                    c, s = turn_ref[phase, 0], turn_ref[phase, 1]
                    real, imag = real * c - imag * s, real * s + imag * c
                z.append((real, imag))
            (ar, ai), (br, bi), (cr, ci), (dr, di) = z
            pr, pi, qr, qi = ar + cr, ai + ci, ar - cr, ai - ci
            ur, ui, vr, vi = br + dr, bi + di, br - dr, bi - di
            reals = (pr + ur, qr + vi, pr - ur, qr - vi)
            imags = (pi + ui, qi - vr, pi - ui, qi + vr)
            for part, values in enumerate((reals, imags)):
                for r, value in enumerate(values):
                    row = turn * length + (at // 8 * 4 + r) * 8
                    os[part, row : row + 8, :] = value
        copies[2 * turn].start()
        copies[2 * turn + 1].start()

    run(0)
    for turn in range(1, turns):
        pl.when(me >= 0)(lambda turn=turn: run(turn))
    for copy in copies:
        copy.wait()


def tables_kernel(spread_hbm, table_hbm, turn_hbm, spread_ref, table_ref, turn_ref, taps_ref, sems):
    copies = [
        pltpu.make_async_copy(source, target, sems.at[i])
        for i, (source, target) in enumerate(((spread_hbm, taps_ref), (table_hbm, table_ref), (turn_hbm, turn_ref)))
    ]
    for copy in copies:
        copy.start()
    for copy in copies:
        copy.wait()
    for phase in range(taps_ref.shape[0]):
        for j in range(taps_ref.shape[1]):
            spread_ref[phase, j] = jnp.broadcast_to(taps_ref[phase, j : j + 1], (8, LANES))


def fine_tables_section(fine_taps):
    taps_count, fine = fine_taps.shape
    taps = fine_taps.reshape(taps_count, LANES, fine // LANES).transpose(2, 0, 1)
    table, turns = fine_tables(fine)
    turns = np.repeat(turns[:, :, None, :], 8, axis=2)
    shape = (fine // LANES, taps_count, 8, LANES)
    return pl.pallas_call(
        tables_kernel,
        out_shape=[
            pltpu.VMEM(shape, F32),
            pltpu.VMEM((2, 2 * LANES, 2 * LANES), BF16),
            pltpu.VMEM(turns.shape, F32),
        ],
        in_specs=[ANY] * 3,
        out_specs=[VMEM] * 3,
        scratch_shapes=[pltpu.VMEM(taps.shape, F32), pltpu.SemaphoreType.DMA((3,))],
        compiler_params=PARAMS,
        cost_estimate=COST,
        name="tables",
    )(taps, in_hbm(jnp.asarray(np.stack(split_table(table)))), in_hbm(jnp.asarray(turns)))


def fine_begin(pieces, taps, axis, groups, shares):
    span = 2 * LANES // groups
    per, frames = span // (4 * shares), 2 * groups
    acc = pl.pallas_call(
        lambda *refs: fine_start_kernel(axis, groups, shares, *refs),
        out_shape=pltpu.VMEM((shares, 4, 2, frames * per, LANES), F32),
        in_specs=[VMEM] * (1 + groups),
        out_specs=VMEM,
        scratch_shapes=[pltpu.VMEM((groups + 1, 2, span, LANES), F32)],
        compiler_params=PARAMS,
        cost_estimate=COST,
        name="fine_start",
    )(in_vmem(taps), *[in_vmem(value) for value in pieces])
    return acc


def fine_section(moved, tables, acc, axis, groups, shares):
    small = 2 * LANES // (groups * shares)
    per, frames = small // 4, 2 * groups
    height = 4 * frames * per
    length = per * frames * 4
    shared = [*tables, acc]
    out = None
    for share in range(shares):
        more = [] if out is None else [out]
        out = pl.pallas_call(
            lambda *refs: fine_kernel(axis, groups, shares, share, *refs),
            out_shape=pltpu.HBM((2, shares * length, LANES), F32),
            in_specs=[VMEM] * (4 + groups) + [ANY] * len(more),
            out_specs=ANY,
            scratch_shapes=[
                pltpu.VMEM((groups, 2, small, LANES), F32),
                pltpu.VMEM((2, 4, 2, frames * per, LANES), F32),
                pltpu.VMEM((height, 2 * LANES), BF16),
                pltpu.VMEM((height, 2 * LANES), BF16),
                pltpu.VMEM((height, 2 * LANES), F32),
                pltpu.VMEM((2, length, LANES), F32),
                pltpu.SemaphoreType.DMA((4,)),
            ],
            input_output_aliases={4 + groups: 0} if more else {},
            compiler_params=PARAMS,
            cost_estimate=COST,
            name="fine",
        )(*[in_vmem(value) for value in shared + list(moved[share])], *more)
    out = out.reshape(2, shares * per, frames // 8, 4, 8, LANES).transpose(0, 1, 2, 4, 3, 5)
    return out.reshape(2, shares * per, frames, 4 * LANES)


def solution(mesh):
    axis = "tm"
    groups = mesh.shape[axis]

    def swap(value, step):
        return lax.ppermute(value, axis, [(i, i ^ step) for i in range(groups)])

    def staged(signal, coarse_taps, fine_taps):
        shares = 1
        first, second = coarse_section(signal, coarse_taps, axis, groups, shares)
        reached = [swap(first[step // 2 + 1], step) for step in range(2, groups, 2)]
        pieces = [first[0], swap(first[1], 1)]
        moved = [
            [second[0], None]
            + [swap(second[share * (groups - 2) + step], step) for step in range(2, groups)]
            for share in range(shares)
        ]
        beside = swap(second[1], 1)
        for row in moved:
            row[1] = beside
        for value in reached:
            half = value[value.shape[0] // 2 - 4 :]
            pieces += [value, swap(half, 1)]
        tables = fine_tables_section(fine_taps)
        acc = fine_begin(pieces, tables[0], axis, groups, shares)
        return fine_section(moved, tables, acc, axis, groups, shares)

    return jax.shard_map(
        staged,
        mesh=mesh,
        in_specs=(P(None, ("streams", "tm")), P(), P()),
        out_specs=P(None, "tm", "streams", None),
        check_vma=False,
    )
```

```python
import math

import jax
import jax.numpy as jnp
import numpy as np
from jax import lax
from jax.experimental import pallas as pl
from jax.experimental.pallas import tpu as pltpu
from jax.sharding import PartitionSpec as P

LANES = 128
F32, BF16 = jnp.float32, jnp.bfloat16


def split_table(table):
    high = np.asarray(table, np.float32).astype(jnp.bfloat16)
    low = (np.asarray(table, np.float64) - high.astype(np.float64)).astype(np.float32).astype(jnp.bfloat16)
    return high, low


def complex_table(turns, points, factor):
    angle = (turns % points) * (2.0 * math.pi / points)
    return np.cos(angle) * factor, -np.sin(angle) * factor


def coarse_table(channels, groups, shares):
    halves, per = LANES // channels, channels // (groups * shares)
    k, p = np.arange(channels), np.arange(channels)
    real, imag = complex_table(k[:, None] * p[None, :], channels, 1.0 / math.sqrt(channels))
    table = np.zeros((groups * shares, 2, halves, per, 2, halves, channels))
    real, imag = real.reshape(-1, per, channels), imag.reshape(-1, per, channels)
    for half in range(halves):
        table[:, 0, half, :, 0, half] = real
        table[:, 0, half, :, 1, half] = -imag
        table[:, 1, half, :, 0, half] = imag
        table[:, 1, half, :, 1, half] = real
    return table.reshape(2 * LANES, 2 * LANES)


def fine_tables(fine):
    radix = fine // LANES
    i = np.arange(LANES)
    real, imag = complex_table(i[:, None] * i[None, :], LANES, 1.0 / math.sqrt(fine))
    table = np.block([[real, imag], [-imag, real]])
    real, imag = complex_table(np.arange(radix)[:, None] * i[None, :], fine, 1.0)
    return table, np.stack([real, imag], axis=1).astype(np.float32)


def split_value(value):
    high = value.astype(BF16)
    return high, (value - high.astype(F32)).astype(BF16)


def dot_nt(left, right):
    return lax.dot_general(left, right, (((1,), (1,)), ((), ())), preferred_element_type=F32)


def dot_nn(left, right):
    return lax.dot_general(left, right, (((1,), (0,)), ((), ())), preferred_element_type=F32)


VMEM = pl.BlockSpec(memory_space=pltpu.VMEM)
ANY = pl.BlockSpec(memory_space=pl.ANY)
PARAMS = pltpu.CompilerParams(vmem_limit_bytes=24 * 1024 * 1024)


def in_vmem(value):
    return pltpu.with_memory_space_constraint(value, pltpu.VMEM)


PAD = 16
PIECES = 4
COST = pl.CostEstimate(flops=2000000, bytes_accessed=1000000, transcendentals=0)


def in_hbm(value):
    return pltpu.with_memory_space_constraint(value, pltpu.HBM)


def pick_rows(table_ref, half, axis, groups, steps):
    me = lax.axis_index(axis)
    span = 2 * LANES // groups
    picks = [pl.multiple_of((me ^ step) * span, span) for step in steps]
    return jnp.concatenate([table_ref[half, pl.ds(pick, span), :] for pick in picks], axis=0)


def filter_rows(xs, ys, bs, taps, base, block, origin):
    channels = LANES // 2
    lower = lax.broadcasted_iota(jnp.int32, (1, LANES), 1) < channels
    now = xs[PAD + base : PAD + base + block]
    before = xs[PAD + base - 2 : PAD + base + block - 2]
    at = base - origin
    ys[PAD + at : PAD + at + block] = pltpu.roll(jnp.where(lower, now, before), channels, 1)
    if bs is None:
        return
    summed = None
    for parity, source, start in ((0, xs, PAD + base), (1, ys, PAD + at)):
        for shift in range(taps.shape[0] // 4):
            low = start - 2 * shift - 8
            piece = source[low : low + block + 8]
            near = taps[2 * shift + parity][None, :]
            far = taps[2 * (shift + 4) + parity][None, :]
            term = piece[8:] * near + piece[:block] * far
            summed = term if summed is None else summed + term
    bs[at : at + block] = summed


def gather_rows(bs, base, count):
    parts = [
        jnp.concatenate([bs[pl.ds(base + 2 * a + part, count, stride=4), :] for part in range(2)], axis=1)
        for a in range(2)
    ]
    return jnp.concatenate(parts, axis=0)


def frame_blocks(span, high, low, bh, bl):
    result = dot_nt(high, bh) + dot_nt(low, bh) + dot_nt(high, bl)
    return [
        [result[at : at + span, a * LANES : (a + 1) * LANES] for a in range(2)]
        for at in range(0, high.shape[0], span)
    ]


def tail_rows(high, low, th, tl):
    tail = dot_nt(th, high) + dot_nt(th, low) + dot_nt(tl, high)
    spare = -tail.shape[1] % LANES
    return jnp.concatenate([tail, jnp.zeros((tail.shape[0], spare), F32)], axis=1) if spare else tail


def coarse_kernel(axis, groups, x_hbm, taps_hbm, table_hbm, *rest):
    lots = groups // 2 - 1
    outs, (bh_ref, bl_ref, th_ref, tl_ref, table_ref, taps_out, xs, taps_ref, ys, bs, xt, yt, bt, sems) = rest[:lots], rest[lots:]
    rows = x_hbm.shape[0]
    span = 2 * LANES // groups
    step = rows // PIECES
    loads = [
        pltpu.make_async_copy(x_hbm.at[pl.ds(i * step, step)], xs.at[pl.ds(PAD + i * step, step)], sems.at[i])
        for i in range(PIECES)
    ]
    get_taps = pltpu.make_async_copy(taps_hbm, taps_ref, sems.at[PIECES])
    get_table = pltpu.make_async_copy(table_hbm, table_ref, sems.at[PIECES + 1])
    ends = 64
    get_ends = pltpu.make_async_copy(x_hbm.at[pl.ds(rows - ends, ends)], xt.at[pl.ds(PAD, ends)], sems.at[PIECES + 2])
    get_taps.start()
    for load in loads[: PIECES // 2]:
        load.start()
    get_table.start()
    get_ends.start()
    for load in loads[PIECES // 2 :]:
        load.start()
    zeros = jnp.zeros((PAD, LANES), F32)
    xs[:PAD] = zeros
    xs[PAD + rows :] = zeros
    ys[:PAD] = zeros
    get_taps.wait()
    taps = taps_ref[...]
    taps = jnp.concatenate([taps, taps], axis=1)
    taps_out[...] = taps
    block = 64
    for i in range(PIECES // 2):
        loads[i].wait()
        for base in range(i * step, (i + 1) * step, block):
            filter_rows(xs, ys, bs, taps, base, block, 0)
    get_table.wait()
    get_ends.wait()
    steps = range(2, groups)
    high, low = [pick_rows(table_ref, half, axis, groups, steps) for half in range(2)]
    bh, bl = split_value(gather_rows(bs, 0, LANES))
    bh_ref[...], bl_ref[...] = bh, bl
    for i, block in enumerate(frame_blocks(span, high, low, bh, bl)):
        for a in range(2):
            at = i % 2 * 2 * span + a * span
            outs[i // 2][at : at + span] = block[a]
    yt[:PAD] = zeros
    xt[PAD + ends :] = zeros
    filter_rows(xt, yt, None, taps, ends - 16, 16, ends - 16)
    filter_rows(xt, yt, bt, taps, ends, 16, ends - 16)
    th, tl = split_value(jnp.concatenate([gather_rows(bt, 16, 4), jnp.zeros((8, 2 * LANES), F32)], axis=0))
    th_ref[...], tl_ref[...] = th, tl
    tail = tail_rows(high, low, th, tl)
    for i, out in enumerate(outs):
        lanes = 2 * i * span // LANES * LANES
        out[4 * span :] = tail[:8, lanes : lanes + LANES]
    for load in loads[PIECES // 2 :]:
        load.wait()


def coarse_rest_kernel(axis, groups, bh_ref, bl_ref, th_ref, tl_ref, table_ref, taps_ref, xs, *rest):
    lots = 1 + groups
    outs, (ys, bs) = rest[:lots], rest[lots:]
    span = 2 * LANES // groups
    rows = xs.shape[0] - 2 * PAD
    taps = taps_ref[...]
    block = 64
    origin = rows // 2 - 16
    filter_rows(xs, ys, None, taps, origin, 16, origin)
    for base in range(rows // 2, rows, block):
        filter_rows(xs, ys, bs, taps, base, block, origin)
    high, low = [pick_rows(table_ref, half, axis, groups, range(groups)) for half in range(2)]
    bh, bl = split_value(gather_rows(bs, 16, LANES))
    for step, block in enumerate(frame_blocks(span, high, low, bh, bl)):
        out, at = (outs[1 + step], 0) if step != 1 else (outs[2], 2 * span)
        for a in range(2):
            out[at + a * span : at + (a + 1) * span] = block[a]
    near_high, near_low = high[: 2 * span], low[: 2 * span]
    tail = tail_rows(near_high, near_low, th_ref[...], tl_ref[...])
    for out, block in zip((outs[0], outs[2]), frame_blocks(span, near_high, near_low, bh_ref[...], bl_ref[...])):
        for a in range(2):
            out[a * span : (a + 1) * span] = block[a]
        out[out.shape[0] - 8 :] = tail[:8, :LANES]


def coarse_section(signal, coarse_taps, axis, groups, shares):
    length = signal.shape[1]
    taps_count, channels = coarse_taps.shape
    count = length // LANES
    rows = signal.reshape(2, count, LANES).transpose(1, 0, 2).reshape(2 * count, LANES)
    table = jnp.asarray(np.stack(split_table(coarse_table(channels, groups, shares))))
    span = 2 * LANES // groups
    lots = groups // 2 - 1
    first = pl.pallas_call(
        lambda *refs: coarse_kernel(axis, groups, *refs),
        out_shape=[pltpu.VMEM((4 * span + 8, LANES), F32)] * lots
        + [pltpu.VMEM((2 * LANES, 2 * LANES), BF16)] * 2
        + [pltpu.VMEM((16, 2 * LANES), BF16)] * 2
        + [
            pltpu.VMEM((2, 2 * LANES, 2 * LANES), BF16),
            pltpu.VMEM((taps_count, LANES), F32),
            pltpu.VMEM((2 * count + 2 * PAD, LANES), F32),
        ],
        in_specs=[ANY] * 3,
        out_specs=[VMEM] * (lots + 7),
        scratch_shapes=[
            pltpu.VMEM((taps_count, channels), F32),
            pltpu.VMEM((count + PAD, LANES), F32),
            pltpu.VMEM((count, LANES), F32),
            pltpu.VMEM((64 + 2 * PAD, LANES), F32),
            pltpu.VMEM((PAD + 32, LANES), F32),
            pltpu.VMEM((32, LANES), F32),
            pltpu.SemaphoreType.DMA((PIECES + 3,)),
        ],
        compiler_params=PARAMS,
        cost_estimate=COST,
        name="coarse",
    )(in_hbm(rows), in_hbm(coarse_taps), in_hbm(table))
    own, pair, late = [pltpu.VMEM((n * span + m, LANES), F32) for n, m in ((2, 8), (4, 8), (2, 0))]
    second = pl.pallas_call(
        lambda *refs: coarse_rest_kernel(axis, groups, *refs),
        out_shape=[own, late, pair] + [late] * (groups - 2),
        in_specs=[VMEM] * 7,
        out_specs=[VMEM] * (1 + groups),
        scratch_shapes=[
            pltpu.VMEM((count + 16 + PAD, LANES), F32),
            pltpu.VMEM((count + 16, LANES), F32),
        ],
        compiler_params=PARAMS,
        cost_estimate=COST,
        name="coarse_rest",
    )(*[in_vmem(value) for value in first[lots:]])
    return first[:lots], second


def terms(xs, taps, parity, m, a, rows):
    reach = [(g, m - 2 * g - parity) for g in range((m - parity) // 2, -1, -1)]
    height = rows.stop - rows.start
    return [xs[g, a, rows] * tiled(taps[j], height) for g, j in reach if j < len(taps)]


def tiled(tap, height):
    return tap[:height] if height <= 8 else jnp.concatenate([tap] * (height // 8), axis=0)


def fine_start_kernel(axis, groups, shares, taps_ref, *refs):
    pieces, (out_ref, xs) = refs[:groups], refs[groups:]
    span = 2 * LANES // groups
    small, per, frames = span // shares, span // (4 * shares), 2 * groups
    me = lax.axis_index(axis)
    for step in range(groups):
        for a in range(2):
            xs[me ^ step, a] = pieces[step][a * span : (a + 1) * span]
    for step in range(groups):
        tail = jnp.transpose(pieces[step][pieces[step].shape[0] - 8 :])
        at = (step - 2 if step > 1 else step) * span % LANES
        tail = tail[at : at + span]
        owner = (me ^ step) + 1
        for a in range(2):
            xs[owner, a, :, 0:4] = xs[owner, a, :, 0:4] + tail[:, 4 * a : 4 * a + 4]
    for a in range(2):
        for h in range(2):
            phase = 2 * a + h
            taps = [taps_ref[phase, j] for j in range(taps_ref.shape[1])]
            for share in range(shares):
                for part in range(2):
                    at = share * small + (2 * part + h) * per
                    for m in range(frames):
                        value = sum(terms(xs, taps, 0, m, a, slice(at, at + per)))
                        out_ref[share, phase, part, m * per : (m + 1) * per] = value


def fine_kernel(axis, groups, shares, share, taps_ref, table_ref, turn_ref, acc_ref, *refs):
    pieces, (out_hbm, xs, fs, yh, yl, zs, os, sem) = refs[:groups], refs[-8:]
    small = 2 * LANES // (groups * shares)
    per, frames = small // 4, 2 * groups
    me = lax.axis_index(axis)
    for step in range(groups):
        base = 2 * small if step == 1 else 0
        for a in range(2):
            xs[me ^ step, a] = pieces[step][base + a * small : base + (a + 1) * small]
    turns = 2 if per >= 16 else 1
    part_of = per // turns
    height = part_of * frames
    length = height * 4
    high, low = table_ref[0], table_ref[1]
    copies = [
        pltpu.make_async_copy(
            os.at[part, pl.ds(turn * length, length)],
            out_hbm.at[part, pl.ds((share * turns + turn) * length, length)],
            sem.at[2 * turn + part],
        )
        for turn in range(turns)
        for part in range(2)
    ]

    def run(turn):
        top = turn * 4 * height
        for a in range(2):
            for h in range(2):
                phase = 2 * a + h
                taps = [taps_ref[phase, j] for j in range(taps_ref.shape[1])]
                columns = []
                for part in range(2):
                    at = (2 * part + h) * per + turn * part_of
                    rows = slice(at, at + part_of)
                    for m in range(frames):
                        at = m * per + turn * part_of
                        value = sum(terms(xs, taps, 1, m, a, rows), acc_ref[share, phase, part, at : at + part_of])
                        at = m * part_of
                        fs[turn, phase, part, at : at + part_of] = value
                    picked = [fs[turn, phase, part, pl.ds(k, frames, stride=part_of), :] for k in range(part_of)]
                    columns.append(jnp.concatenate(picked, axis=0))
                first, second = split_value(jnp.concatenate(columns, axis=1))
                at = top + phase * height
                yh[at : at + height] = first
                yl[at : at + height] = second
        left, right = yh[top : top + 4 * height], yl[top : top + 4 * height]
        zs[top : top + 4 * height] = dot_nn(left, high) + dot_nn(right, high) + dot_nn(left, low)
        for at in range(0, height, 8):
            z = []
            for phase in range(4):
                row = top + phase * height + at
                real, imag = zs[row : row + 8, :LANES], zs[row : row + 8, LANES:]
                if phase:
                    c, s = turn_ref[phase, 0], turn_ref[phase, 1]
                    real, imag = real * c - imag * s, real * s + imag * c
                z.append((real, imag))
            (ar, ai), (br, bi), (cr, ci), (dr, di) = z
            pr, pi, qr, qi = ar + cr, ai + ci, ar - cr, ai - ci
            ur, ui, vr, vi = br + dr, bi + di, br - dr, bi - di
            reals = (pr + ur, qr + vi, pr - ur, qr - vi)
            imags = (pi + ui, qi - vr, pi - ui, qi + vr)
            for part, values in enumerate((reals, imags)):
                for r, value in enumerate(values):
                    row = turn * length + (at // 8 * 4 + r) * 8
                    os[part, row : row + 8, :] = value
        copies[2 * turn].start()
        copies[2 * turn + 1].start()

    run(0)
    for turn in range(1, turns):
        run(turn)
    for copy in copies:
        copy.wait()


def tables_kernel(spread_hbm, table_hbm, turn_hbm, spread_ref, table_ref, turn_ref, taps_ref, sems):
    copies = [
        pltpu.make_async_copy(source, target, sems.at[i])
        for i, (source, target) in enumerate(((spread_hbm, taps_ref), (table_hbm, table_ref), (turn_hbm, turn_ref)))
    ]
    for copy in copies:
        copy.start()
    for copy in copies:
        copy.wait()
    for phase in range(taps_ref.shape[0]):
        for j in range(taps_ref.shape[1]):
            spread_ref[phase, j] = jnp.broadcast_to(taps_ref[phase, j : j + 1], (8, LANES))


def fine_tables_section(fine_taps):
    taps_count, fine = fine_taps.shape
    taps = fine_taps.reshape(taps_count, LANES, fine // LANES).transpose(2, 0, 1)
    table, turns = fine_tables(fine)
    turns = np.repeat(turns[:, :, None, :], 8, axis=2)
    shape = (fine // LANES, taps_count, 8, LANES)
    return pl.pallas_call(
        tables_kernel,
        out_shape=[
            pltpu.VMEM(shape, F32),
            pltpu.VMEM((2, 2 * LANES, 2 * LANES), BF16),
            pltpu.VMEM(turns.shape, F32),
        ],
        in_specs=[ANY] * 3,
        out_specs=[VMEM] * 3,
        scratch_shapes=[pltpu.VMEM(taps.shape, F32), pltpu.SemaphoreType.DMA((3,))],
        compiler_params=PARAMS,
        cost_estimate=COST,
        name="tables",
    )(taps, in_hbm(jnp.asarray(np.stack(split_table(table)))), in_hbm(jnp.asarray(turns)))


def fine_begin(pieces, taps, axis, groups, shares):
    span = 2 * LANES // groups
    per, frames = span // (4 * shares), 2 * groups
    acc = pl.pallas_call(
        lambda *refs: fine_start_kernel(axis, groups, shares, *refs),
        out_shape=pltpu.VMEM((shares, 4, 2, frames * per, LANES), F32),
        in_specs=[VMEM] * (1 + groups),
        out_specs=VMEM,
        scratch_shapes=[pltpu.VMEM((groups + 1, 2, span, LANES), F32)],
        compiler_params=PARAMS,
        cost_estimate=COST,
        name="fine_start",
    )(in_vmem(taps), *[in_vmem(value) for value in pieces])
    return acc


def fine_section(moved, tables, acc, axis, groups, shares):
    small = 2 * LANES // (groups * shares)
    per, frames = small // 4, 2 * groups
    height = 4 * frames * per
    length = per * frames * 4
    shared = [*tables, acc]
    out = None
    for share in range(shares):
        more = [] if out is None else [out]
        out = pl.pallas_call(
            lambda *refs: fine_kernel(axis, groups, shares, share, *refs),
            out_shape=pltpu.HBM((2, shares * length, LANES), F32),
            in_specs=[VMEM] * (4 + groups) + [ANY] * len(more),
            out_specs=ANY,
            scratch_shapes=[
                pltpu.VMEM((groups, 2, small, LANES), F32),
                pltpu.VMEM((2, 4, 2, frames * per, LANES), F32),
                pltpu.VMEM((height, 2 * LANES), BF16),
                pltpu.VMEM((height, 2 * LANES), BF16),
                pltpu.VMEM((height, 2 * LANES), F32),
                pltpu.VMEM((2, length, LANES), F32),
                pltpu.SemaphoreType.DMA((4,)),
            ],
            input_output_aliases={4 + groups: 0} if more else {},
            compiler_params=PARAMS,
            cost_estimate=COST,
            name="fine",
        )(*[in_vmem(value) for value in shared + list(moved[share])], *more)
    out = out.reshape(2, shares * per, frames // 8, 4, 8, LANES).transpose(0, 1, 2, 4, 3, 5)
    return out.reshape(2, shares * per, frames, 4 * LANES)


def solution(mesh):
    axis = "tm"
    groups = mesh.shape[axis]

    def swap(value, step):
        return lax.ppermute(value, axis, [(i, i ^ step) for i in range(groups)])

    def staged(signal, coarse_taps, fine_taps):
        shares = 1
        first, second = coarse_section(signal, coarse_taps, axis, groups, shares)
        reached = [swap(value, 2 * i + 2) for i, value in enumerate(first)]
        late = [swap(second[1 + step], step) for step in range(2, groups)]
        beside = swap(second[2], 1)
        moved = [[second[1], beside] + late]
        pieces = [second[0], beside]
        for value in reached:
            half = value[value.shape[0] // 2 - 4 :]
            pieces += [value, swap(half, 1)]
        tables = fine_tables_section(fine_taps)
        acc = fine_begin(pieces, tables[0], axis, groups, shares)
        return fine_section(moved, tables, acc, axis, groups, shares)

    return jax.shard_map(
        staged,
        mesh=mesh,
        in_specs=(P(None, ("streams", "tm")), P(), P()),
        out_specs=P(None, "tm", "streams", None),
        check_vma=False,
    )
```

```python
import math

import jax
import jax.numpy as jnp
import numpy as np
from jax import lax
from jax.experimental import pallas as pl
from jax.experimental.pallas import tpu as pltpu
from jax.sharding import PartitionSpec as P

LANES = 128
F32, BF16 = jnp.float32, jnp.bfloat16


def split_table(table):
    high = np.asarray(table, np.float32).astype(jnp.bfloat16)
    low = (np.asarray(table, np.float64) - high.astype(np.float64)).astype(np.float32).astype(jnp.bfloat16)
    return high, low


def complex_table(turns, points, factor):
    angle = (turns % points) * (2.0 * math.pi / points)
    return np.cos(angle) * factor, -np.sin(angle) * factor


def coarse_table(channels, groups, shares):
    halves, per = LANES // channels, channels // (groups * shares)
    k, p = np.arange(channels), np.arange(channels)
    real, imag = complex_table(k[:, None] * p[None, :], channels, 1.0 / math.sqrt(channels))
    table = np.zeros((groups * shares, 2, halves, per, 2, halves, channels))
    real, imag = real.reshape(-1, per, channels), imag.reshape(-1, per, channels)
    for half in range(halves):
        table[:, 0, half, :, 0, half] = real
        table[:, 0, half, :, 1, half] = -imag
        table[:, 1, half, :, 0, half] = imag
        table[:, 1, half, :, 1, half] = real
    return table.reshape(2 * LANES, 2 * LANES)


def fine_tables(fine):
    radix = fine // LANES
    i = np.arange(LANES)
    real, imag = complex_table(i[:, None] * i[None, :], LANES, 1.0 / math.sqrt(fine))
    table = np.block([[real, imag], [-imag, real]])
    real, imag = complex_table(np.arange(radix)[:, None] * i[None, :], fine, 1.0)
    return table, np.stack([real, imag], axis=1).astype(np.float32)


def split_value(value):
    high = value.astype(BF16)
    return high, (value - high.astype(F32)).astype(BF16)


def dot_nt(left, right):
    return lax.dot_general(left, right, (((1,), (1,)), ((), ())), preferred_element_type=F32)


def dot_nn(left, right):
    return lax.dot_general(left, right, (((1,), (0,)), ((), ())), preferred_element_type=F32)


VMEM = pl.BlockSpec(memory_space=pltpu.VMEM)
ANY = pl.BlockSpec(memory_space=pl.ANY)
PARAMS = pltpu.CompilerParams(vmem_limit_bytes=24 * 1024 * 1024)


def in_vmem(value):
    return pltpu.with_memory_space_constraint(value, pltpu.VMEM)


PAD = 16
PIECES = 4
COST = pl.CostEstimate(flops=2000000, bytes_accessed=1000000, transcendentals=0)


def in_hbm(value):
    return pltpu.with_memory_space_constraint(value, pltpu.HBM)


def pick_rows(table_ref, half, axis, groups, steps):
    me = lax.axis_index(axis)
    span = 2 * LANES // groups
    picks = [pl.multiple_of((me ^ step) * span, span) for step in steps]
    return jnp.concatenate([table_ref[half, pl.ds(pick, span), :] for pick in picks], axis=0)


def filter_rows(xs, ys, bs, taps, base, block, origin):
    channels = LANES // 2
    lower = lax.broadcasted_iota(jnp.int32, (1, LANES), 1) < channels
    now = xs[PAD + base : PAD + base + block]
    before = xs[PAD + base - 2 : PAD + base + block - 2]
    at = base - origin
    ys[PAD + at : PAD + at + block] = pltpu.roll(jnp.where(lower, now, before), channels, 1)
    if bs is None:
        return
    summed = None
    for parity, source, start in ((0, xs, PAD + base), (1, ys, PAD + at)):
        for shift in range(taps.shape[0] // 4):
            low = start - 2 * shift - 8
            piece = source[low : low + block + 8]
            near = taps[2 * shift + parity][None, :]
            far = taps[2 * (shift + 4) + parity][None, :]
            term = piece[8:] * near + piece[:block] * far
            summed = term if summed is None else summed + term
    bs[at : at + block] = summed


def gather_rows(bs, base, count):
    parts = [
        jnp.concatenate([bs[pl.ds(base + 2 * a + part, count, stride=4), :] for part in range(2)], axis=1)
        for a in range(2)
    ]
    return jnp.concatenate(parts, axis=0)


def frame_blocks(span, high, low, bh, bl):
    result = dot_nt(high, bh) + dot_nt(low, bh) + dot_nt(high, bl)
    return [
        [result[at : at + span, a * LANES : (a + 1) * LANES] for a in range(2)]
        for at in range(0, high.shape[0], span)
    ]


def tail_rows(high, low, th, tl):
    tail = dot_nt(th, high) + dot_nt(th, low) + dot_nt(tl, high)
    spare = -tail.shape[1] % LANES
    return jnp.concatenate([tail, jnp.zeros((tail.shape[0], spare), F32)], axis=1) if spare else tail


def coarse_kernel(axis, groups, x_hbm, taps_hbm, table_hbm, *rest):
    lots = groups // 2 - 1
    outs, (bh_ref, bl_ref, th_ref, tl_ref, table_ref, taps_out, xs, taps_ref, ys, bs, xt, yt, bt, sems) = rest[:lots], rest[lots:]
    rows = x_hbm.shape[0]
    span = 2 * LANES // groups
    step = rows // PIECES
    loads = [
        pltpu.make_async_copy(x_hbm.at[pl.ds(i * step, step)], xs.at[pl.ds(PAD + i * step, step)], sems.at[i])
        for i in range(PIECES)
    ]
    get_taps = pltpu.make_async_copy(taps_hbm, taps_ref, sems.at[PIECES])
    get_table = pltpu.make_async_copy(table_hbm, table_ref, sems.at[PIECES + 1])
    ends = 64
    get_ends = pltpu.make_async_copy(x_hbm.at[pl.ds(rows - ends, ends)], xt.at[pl.ds(PAD, ends)], sems.at[PIECES + 2])
    get_taps.start()
    for load in loads[: PIECES // 2]:
        load.start()
    get_table.start()
    get_ends.start()
    for load in loads[PIECES // 2 :]:
        load.start()
    zeros = jnp.zeros((PAD, LANES), F32)
    xs[:PAD] = zeros
    xs[PAD + rows :] = zeros
    ys[:PAD] = zeros
    get_taps.wait()
    taps = taps_ref[...]
    taps = jnp.concatenate([taps, taps], axis=1)
    taps_out[...] = taps
    block = 64
    for i in range(PIECES // 2):
        loads[i].wait()
        for base in range(i * step, (i + 1) * step, block):
            filter_rows(xs, ys, bs, taps, base, block, 0)
    get_table.wait()
    get_ends.wait()
    steps = range(2, groups)
    high, low = [pick_rows(table_ref, half, axis, groups, steps) for half in range(2)]
    bh, bl = split_value(gather_rows(bs, 0, LANES))
    bh_ref[...], bl_ref[...] = bh, bl
    for i, block in enumerate(frame_blocks(span, high, low, bh, bl)):
        for a in range(2):
            at = i % 2 * 2 * span + a * span
            outs[i // 2][at : at + span] = block[a]
    yt[:PAD] = zeros
    xt[PAD + ends :] = zeros
    filter_rows(xt, yt, None, taps, ends - 16, 16, ends - 16)
    filter_rows(xt, yt, bt, taps, ends, 16, ends - 16)
    th, tl = split_value(jnp.concatenate([gather_rows(bt, 16, 4), jnp.zeros((8, 2 * LANES), F32)], axis=0))
    th_ref[...], tl_ref[...] = th, tl
    tail = tail_rows(high, low, th, tl)
    for i, out in enumerate(outs):
        lanes = 2 * i * span // LANES * LANES
        out[4 * span :] = tail[:8, lanes : lanes + LANES]
    for load in loads[PIECES // 2 :]:
        load.wait()


def coarse_rest_kernel(axis, groups, bh_ref, bl_ref, th_ref, tl_ref, table_ref, taps_ref, xs, *rest):
    lots = 1 + groups
    outs, (ys, bs) = rest[:lots], rest[lots:]
    span = 2 * LANES // groups
    rows = xs.shape[0] - 2 * PAD
    taps = taps_ref[...]
    block = 64
    origin = rows // 2 - 16
    filter_rows(xs, ys, None, taps, origin, 16, origin)
    for base in range(rows // 2, rows, block):
        filter_rows(xs, ys, bs, taps, base, block, origin)
    high, low = [pick_rows(table_ref, half, axis, groups, range(groups)) for half in range(2)]
    bh, bl = split_value(gather_rows(bs, 16, LANES))
    for step, block in enumerate(frame_blocks(span, high, low, bh, bl)):
        out, at = (outs[1 + step], 0) if step != 1 else (outs[2], 2 * span)
        for a in range(2):
            out[at + a * span : at + (a + 1) * span] = block[a]
    near_high, near_low = high[: 2 * span], low[: 2 * span]
    tail = tail_rows(near_high, near_low, th_ref[...], tl_ref[...])
    for out, block in zip((outs[0], outs[2]), frame_blocks(span, near_high, near_low, bh_ref[...], bl_ref[...])):
        for a in range(2):
            out[a * span : (a + 1) * span] = block[a]
        out[out.shape[0] - 8 :] = tail[:8, :LANES]


def coarse_section(signal, coarse_taps, axis, groups, shares):
    length = signal.shape[1]
    taps_count, channels = coarse_taps.shape
    count = length // LANES
    rows = signal.reshape(2, count, LANES).transpose(1, 0, 2).reshape(2 * count, LANES)
    table = jnp.asarray(np.stack(split_table(coarse_table(channels, groups, shares))))
    span = 2 * LANES // groups
    lots = groups // 2 - 1
    first = pl.pallas_call(
        lambda *refs: coarse_kernel(axis, groups, *refs),
        out_shape=[pltpu.VMEM((4 * span + 8, LANES), F32)] * lots
        + [pltpu.VMEM((2 * LANES, 2 * LANES), BF16)] * 2
        + [pltpu.VMEM((16, 2 * LANES), BF16)] * 2
        + [
            pltpu.VMEM((2, 2 * LANES, 2 * LANES), BF16),
            pltpu.VMEM((taps_count, LANES), F32),
            pltpu.VMEM((2 * count + 2 * PAD, LANES), F32),
        ],
        in_specs=[ANY] * 3,
        out_specs=[VMEM] * (lots + 7),
        scratch_shapes=[
            pltpu.VMEM((taps_count, channels), F32),
            pltpu.VMEM((count + PAD, LANES), F32),
            pltpu.VMEM((count, LANES), F32),
            pltpu.VMEM((64 + 2 * PAD, LANES), F32),
            pltpu.VMEM((PAD + 32, LANES), F32),
            pltpu.VMEM((32, LANES), F32),
            pltpu.SemaphoreType.DMA((PIECES + 3,)),
        ],
        compiler_params=PARAMS,
        cost_estimate=COST,
        name="coarse",
    )(in_hbm(rows), in_hbm(coarse_taps), in_hbm(table))
    own, pair, late = [pltpu.VMEM((n * span + m, LANES), F32) for n, m in ((2, 8), (4, 8), (2, 0))]
    second = pl.pallas_call(
        lambda *refs: coarse_rest_kernel(axis, groups, *refs),
        out_shape=[own, late, pair] + [late] * (groups - 2),
        in_specs=[VMEM] * 7,
        out_specs=[VMEM] * (1 + groups),
        scratch_shapes=[
            pltpu.VMEM((count + 16 + PAD, LANES), F32),
            pltpu.VMEM((count + 16, LANES), F32),
        ],
        compiler_params=PARAMS,
        cost_estimate=COST,
        name="coarse_rest",
    )(*[in_vmem(value) for value in first[lots:]])
    return first[:lots], second


def terms(xs, taps, parity, m, a, rows):
    reach = [(g, m - 2 * g - parity) for g in range((m - parity) // 2, -1, -1)]
    height = rows.stop - rows.start
    return [xs[g, a, rows] * tiled(taps[j], height) for g, j in reach if j < len(taps)]


def tiled(tap, height):
    return tap[:height] if height <= 8 else jnp.concatenate([tap] * (height // 8), axis=0)


def add_piece(axis, groups, piece, step, xs):
    span = 2 * LANES // groups
    owner = lax.axis_index(axis) ^ step
    at = (step - 2 if step > 1 else step) * span % LANES
    tail = jnp.transpose(piece[piece.shape[0] - 8 :])[at : at + span]
    for a in range(2):
        xs[owner, a] = xs[owner, a] + piece[a * span : (a + 1) * span]
        xs[owner + 1, a, :, 0:4] = xs[owner + 1, a, :, 0:4] + tail[:, 4 * a : 4 * a + 4]


def fine_start_kernel(axis, groups, shares, taps_ref, near_ref, *refs):
    steps = range(3, groups, 2)
    pieces, (out_ref, xs) = refs[: len(steps)], refs[len(steps) :]
    span = 2 * LANES // groups
    small, per, frames = span // shares, span // (4 * shares), 2 * groups
    xs[...] = near_ref[...]
    for step, piece in zip(steps, pieces):
        add_piece(axis, groups, piece, step, xs)
    for a in range(2):
        for h in range(2):
            phase = 2 * a + h
            taps = [taps_ref[phase, j] for j in range(taps_ref.shape[1])]
            for share in range(shares):
                for part in range(2):
                    at = share * small + (2 * part + h) * per
                    for m in range(frames):
                        value = sum(terms(xs, taps, 0, m, a, slice(at, at + per)))
                        out_ref[share, phase, part, m * per : (m + 1) * per] = value


def fine_kernel(axis, groups, shares, share, taps_ref, table_ref, turn_ref, acc_ref, *refs):
    pieces, (out_hbm, xs, fs, yh, yl, zs, os, sem) = refs[:groups], refs[-8:]
    small = 2 * LANES // (groups * shares)
    per, frames = small // 4, 2 * groups
    me = lax.axis_index(axis)
    for step in range(groups):
        base = 2 * small if step == 1 else 0
        for a in range(2):
            xs[me ^ step, a] = pieces[step][base + a * small : base + (a + 1) * small]
    turns = 2 if per >= 16 else 1
    part_of = per // turns
    height = part_of * frames
    length = height * 4
    high, low = table_ref[0], table_ref[1]
    copies = [
        pltpu.make_async_copy(
            os.at[part, pl.ds(turn * length, length)],
            out_hbm.at[part, pl.ds((share * turns + turn) * length, length)],
            sem.at[2 * turn + part],
        )
        for turn in range(turns)
        for part in range(2)
    ]

    def run(turn):
        top = turn * 4 * height
        for a in range(2):
            for h in range(2):
                phase = 2 * a + h
                taps = [taps_ref[phase, j] for j in range(taps_ref.shape[1])]
                columns = []
                for part in range(2):
                    at = (2 * part + h) * per + turn * part_of
                    rows = slice(at, at + part_of)
                    for m in range(frames):
                        at = m * per + turn * part_of
                        value = sum(terms(xs, taps, 1, m, a, rows), acc_ref[share, phase, part, at : at + part_of])
                        at = m * part_of
                        fs[turn, phase, part, at : at + part_of] = value
                    picked = [fs[turn, phase, part, pl.ds(k, frames, stride=part_of), :] for k in range(part_of)]
                    columns.append(jnp.concatenate(picked, axis=0))
                first, second = split_value(jnp.concatenate(columns, axis=1))
                at = top + phase * height
                yh[at : at + height] = first
                yl[at : at + height] = second
        left, right = yh[top : top + 4 * height], yl[top : top + 4 * height]
        zs[top : top + 4 * height] = dot_nn(left, high) + dot_nn(right, high) + dot_nn(left, low)
        for at in range(0, height, 8):
            z = []
            for phase in range(4):
                row = top + phase * height + at
                real, imag = zs[row : row + 8, :LANES], zs[row : row + 8, LANES:]
                if phase:
                    c, s = turn_ref[phase, 0], turn_ref[phase, 1]
                    real, imag = real * c - imag * s, real * s + imag * c
                z.append((real, imag))
            (ar, ai), (br, bi), (cr, ci), (dr, di) = z
            pr, pi, qr, qi = ar + cr, ai + ci, ar - cr, ai - ci
            ur, ui, vr, vi = br + dr, bi + di, br - dr, bi - di
            reals = (pr + ur, qr + vi, pr - ur, qr - vi)
            imags = (pi + ui, qi - vr, pi - ui, qi + vr)
            for part, values in enumerate((reals, imags)):
                for r, value in enumerate(values):
                    row = turn * length + (at // 8 * 4 + r) * 8
                    os[part, row : row + 8, :] = value
        copies[2 * turn].start()
        copies[2 * turn + 1].start()

    run(0)
    for turn in range(1, turns):
        run(turn)
    for copy in copies:
        copy.wait()


def tables_kernel(axis, groups, spread_hbm, table_hbm, turn_hbm, *refs):
    steps = [0, 1, *range(2, groups, 2)]
    pieces, (spread_ref, table_ref, turn_ref, near_ref, taps_ref, sems) = refs[: len(steps)], refs[len(steps) :]
    copies = [
        pltpu.make_async_copy(source, target, sems.at[i])
        for i, (source, target) in enumerate(((spread_hbm, taps_ref), (table_hbm, table_ref), (turn_hbm, turn_ref)))
    ]
    for copy in copies:
        copy.start()
    near_ref[...] = jnp.zeros_like(near_ref)
    for step, piece in zip(steps, pieces):
        add_piece(axis, groups, piece, step, near_ref)
    for copy in copies:
        copy.wait()
    for phase in range(taps_ref.shape[0]):
        for j in range(taps_ref.shape[1]):
            spread_ref[phase, j] = jnp.broadcast_to(taps_ref[phase, j : j + 1], (8, LANES))


def fine_tables_section(pieces, fine_taps, axis, groups):
    taps_count, fine = fine_taps.shape
    taps = fine_taps.reshape(taps_count, LANES, fine // LANES).transpose(2, 0, 1)
    table, turns = fine_tables(fine)
    turns = np.repeat(turns[:, :, None, :], 8, axis=2)
    shape = (fine // LANES, taps_count, 8, LANES)
    return pl.pallas_call(
        lambda *refs: tables_kernel(axis, groups, *refs),
        out_shape=[
            pltpu.VMEM(shape, F32),
            pltpu.VMEM((2, 2 * LANES, 2 * LANES), BF16),
            pltpu.VMEM(turns.shape, F32),
            pltpu.VMEM((groups + 1, 2, 2 * LANES // groups, LANES), F32),
        ],
        in_specs=[ANY] * 3 + [VMEM] * len(pieces),
        out_specs=[VMEM] * 4,
        scratch_shapes=[pltpu.VMEM(taps.shape, F32), pltpu.SemaphoreType.DMA((3,))],
        compiler_params=PARAMS,
        cost_estimate=COST,
        name="tables",
    )(taps, in_hbm(jnp.asarray(np.stack(split_table(table)))), in_hbm(jnp.asarray(turns)), *map(in_vmem, pieces))


def fine_begin(pieces, near, taps, axis, groups, shares):
    span = 2 * LANES // groups
    per, frames = span // (4 * shares), 2 * groups
    acc = pl.pallas_call(
        lambda *refs: fine_start_kernel(axis, groups, shares, *refs),
        out_shape=pltpu.VMEM((shares, 4, 2, frames * per, LANES), F32),
        in_specs=[VMEM] * (2 + len(pieces)),
        out_specs=VMEM,
        scratch_shapes=[pltpu.VMEM((groups + 1, 2, span, LANES), F32)],
        compiler_params=PARAMS,
        cost_estimate=COST,
        name="fine_start",
    )(in_vmem(taps), in_vmem(near), *[in_vmem(value) for value in pieces])
    return acc


def fine_section(moved, tables, acc, axis, groups, shares):
    small = 2 * LANES // (groups * shares)
    per, frames = small // 4, 2 * groups
    height = 4 * frames * per
    length = per * frames * 4
    shared = [*tables, acc]
    out = None
    for share in range(shares):
        more = [] if out is None else [out]
        out = pl.pallas_call(
            lambda *refs: fine_kernel(axis, groups, shares, share, *refs),
            out_shape=pltpu.HBM((2, shares * length, LANES), F32),
            in_specs=[VMEM] * (4 + groups) + [ANY] * len(more),
            out_specs=ANY,
            scratch_shapes=[
                pltpu.VMEM((groups, 2, small, LANES), F32),
                pltpu.VMEM((2, 4, 2, frames * per, LANES), F32),
                pltpu.VMEM((height, 2 * LANES), BF16),
                pltpu.VMEM((height, 2 * LANES), BF16),
                pltpu.VMEM((height, 2 * LANES), F32),
                pltpu.VMEM((2, length, LANES), F32),
                pltpu.SemaphoreType.DMA((4,)),
            ],
            input_output_aliases={4 + groups: 0} if more else {},
            compiler_params=PARAMS,
            cost_estimate=COST,
            name="fine",
        )(*[in_vmem(value) for value in shared + list(moved[share])], *more)
    out = out.reshape(2, shares * per, frames // 8, 4, 8, LANES).transpose(0, 1, 2, 4, 3, 5)
    return out.reshape(2, shares * per, frames, 4 * LANES)


def solution(mesh):
    axis = "tm"
    groups = mesh.shape[axis]

    def swap(value, step):
        return lax.ppermute(value, axis, [(i, i ^ step) for i in range(groups)])

    def staged(signal, coarse_taps, fine_taps):
        shares = 1
        first, second = coarse_section(signal, coarse_taps, axis, groups, shares)
        reached = [swap(value, 2 * i + 2) for i, value in enumerate(first)]
        late = [swap(second[1 + step], step) for step in range(2, groups)]
        beside = swap(second[2], 1)
        moved = [[second[1], beside] + late]
        relayed = []
        for value in reached:
            half = value[value.shape[0] // 2 - 4 :]
            relayed.append(swap(half, 1))
        *tables, near = fine_tables_section([second[0], beside, *reached], fine_taps, axis, groups)
        acc = fine_begin(relayed, near, tables[0], axis, groups, shares)
        return fine_section(moved, tables, acc, axis, groups, shares)

    return jax.shard_map(
        staged,
        mesh=mesh,
        in_specs=(P(None, ("streams", "tm")), P(), P()),
        out_specs=P(None, "tm", "streams", None),
        check_vma=False,
    )
```

```python
import math

import jax
import jax.numpy as jnp
import numpy as np
from jax import lax
from jax.experimental import pallas as pl
from jax.experimental.pallas import tpu as pltpu
from jax.sharding import PartitionSpec as P

LANES = 128
F32, BF16 = jnp.float32, jnp.bfloat16


def split_table(table):
    high = np.asarray(table, np.float32).astype(jnp.bfloat16)
    low = (np.asarray(table, np.float64) - high.astype(np.float64)).astype(np.float32).astype(jnp.bfloat16)
    return high, low


def complex_table(turns, points, factor):
    angle = (turns % points) * (2.0 * math.pi / points)
    return np.cos(angle) * factor, -np.sin(angle) * factor


def coarse_table(channels, groups, shares):
    halves, per = LANES // channels, channels // (groups * shares)
    k, p = np.arange(channels), np.arange(channels)
    real, imag = complex_table(k[:, None] * p[None, :], channels, 1.0 / math.sqrt(channels))
    table = np.zeros((groups * shares, 2, halves, per, 2, halves, channels))
    real, imag = real.reshape(-1, per, channels), imag.reshape(-1, per, channels)
    for half in range(halves):
        table[:, 0, half, :, 0, half] = real
        table[:, 0, half, :, 1, half] = -imag
        table[:, 1, half, :, 0, half] = imag
        table[:, 1, half, :, 1, half] = real
    return table.reshape(2 * LANES, 2 * LANES)


def fine_tables(fine):
    radix = fine // LANES
    i = np.arange(LANES)
    real, imag = complex_table(i[:, None] * i[None, :], LANES, 1.0 / math.sqrt(fine))
    table = np.block([[real, imag], [-imag, real]])
    real, imag = complex_table(np.arange(radix)[:, None] * i[None, :], fine, 1.0)
    return table, np.stack([real, imag], axis=1).astype(np.float32)


def split_value(value):
    high = value.astype(BF16)
    return high, (value - high.astype(F32)).astype(BF16)


def dot_nt(left, right):
    return lax.dot_general(left, right, (((1,), (1,)), ((), ())), preferred_element_type=F32)


def dot_nn(left, right):
    return lax.dot_general(left, right, (((1,), (0,)), ((), ())), preferred_element_type=F32)


VMEM = pl.BlockSpec(memory_space=pltpu.VMEM)
ANY = pl.BlockSpec(memory_space=pl.ANY)
PARAMS = pltpu.CompilerParams(vmem_limit_bytes=24 * 1024 * 1024)


def in_vmem(value):
    return pltpu.with_memory_space_constraint(value, pltpu.VMEM)


PAD = 16
PIECES = 4
COST = pl.CostEstimate(flops=2000000, bytes_accessed=1000000, transcendentals=0)


def in_hbm(value):
    return pltpu.with_memory_space_constraint(value, pltpu.HBM)


def pick_rows(table_ref, half, axis, groups, steps):
    me = lax.axis_index(axis)
    span = 2 * LANES // groups
    picks = [pl.multiple_of((me ^ step) * span, span) for step in steps]
    return jnp.concatenate([table_ref[half, pl.ds(pick, span), :] for pick in picks], axis=0)


def filter_rows(xs, ys, bs, taps, base, block, origin):
    channels = LANES // 2
    lower = lax.broadcasted_iota(jnp.int32, (1, LANES), 1) < channels
    now = xs[PAD + base : PAD + base + block]
    before = xs[PAD + base - 2 : PAD + base + block - 2]
    at = base - origin
    ys[PAD + at : PAD + at + block] = pltpu.roll(jnp.where(lower, now, before), channels, 1)
    if bs is None:
        return
    summed = None
    for parity, source, start in ((0, xs, PAD + base), (1, ys, PAD + at)):
        for shift in range(taps.shape[0] // 4):
            low = start - 2 * shift - 8
            piece = source[low : low + block + 8]
            near = taps[2 * shift + parity][None, :]
            far = taps[2 * (shift + 4) + parity][None, :]
            term = piece[8:] * near + piece[:block] * far
            summed = term if summed is None else summed + term
    bs[at : at + block] = summed


def gather_rows(bs, base, count):
    parts = [
        jnp.concatenate([bs[pl.ds(base + 2 * a + part, count, stride=4), :] for part in range(2)], axis=1)
        for a in range(2)
    ]
    return jnp.concatenate(parts, axis=0)


def frame_blocks(span, high, low, bh, bl):
    result = dot_nt(high, bh) + dot_nt(low, bh) + dot_nt(high, bl)
    return [
        [result[at : at + span, a * LANES : (a + 1) * LANES] for a in range(2)]
        for at in range(0, high.shape[0], span)
    ]


def tail_rows(high, low, th, tl):
    tail = dot_nt(th, high) + dot_nt(th, low) + dot_nt(tl, high)
    spare = -tail.shape[1] % LANES
    return jnp.concatenate([tail, jnp.zeros((tail.shape[0], spare), F32)], axis=1) if spare else tail


def coarse_kernel(axis, groups, x_hbm, taps_hbm, table_hbm, *rest):
    lots = groups // 2 - 1
    outs, (bh_ref, bl_ref, th_ref, tl_ref, table_ref, taps_out, xs, taps_ref, ys, bs, xt, yt, bt, sems) = rest[:lots], rest[lots:]
    rows = x_hbm.shape[0]
    span = 2 * LANES // groups
    step = rows // PIECES
    loads = [
        pltpu.make_async_copy(x_hbm.at[pl.ds(i * step, step)], xs.at[pl.ds(PAD + i * step, step)], sems.at[i])
        for i in range(PIECES)
    ]
    get_taps = pltpu.make_async_copy(taps_hbm, taps_ref, sems.at[PIECES])
    get_table = pltpu.make_async_copy(table_hbm, table_ref, sems.at[PIECES + 1])
    ends = 64
    get_ends = pltpu.make_async_copy(x_hbm.at[pl.ds(rows - ends, ends)], xt.at[pl.ds(PAD, ends)], sems.at[PIECES + 2])
    get_taps.start()
    for load in loads[: PIECES // 2]:
        load.start()
    get_table.start()
    get_ends.start()
    for load in loads[PIECES // 2 :]:
        load.start()
    zeros = jnp.zeros((PAD, LANES), F32)
    xs[:PAD] = zeros
    xs[PAD + rows :] = zeros
    ys[:PAD] = zeros
    get_taps.wait()
    taps = taps_ref[...]
    taps = jnp.concatenate([taps, taps], axis=1)
    taps_out[...] = taps
    block = 64
    for i in range(PIECES // 2):
        loads[i].wait()
        for base in range(i * step, (i + 1) * step, block):
            filter_rows(xs, ys, bs, taps, base, block, 0)
    get_table.wait()
    get_ends.wait()
    steps = range(2, groups)
    high, low = [pick_rows(table_ref, half, axis, groups, steps) for half in range(2)]
    bh, bl = split_value(gather_rows(bs, 0, LANES))
    bh_ref[...], bl_ref[...] = bh, bl
    for i, block in enumerate(frame_blocks(span, high, low, bh, bl)):
        for a in range(2):
            at = i % 2 * 2 * span + a * span
            outs[i // 2][at : at + span] = block[a]
    yt[:PAD] = zeros
    xt[PAD + ends :] = zeros
    filter_rows(xt, yt, None, taps, ends - 16, 16, ends - 16)
    filter_rows(xt, yt, bt, taps, ends, 16, ends - 16)
    th, tl = split_value(jnp.concatenate([gather_rows(bt, 16, 4), jnp.zeros((8, 2 * LANES), F32)], axis=0))
    th_ref[...], tl_ref[...] = th, tl
    tail = tail_rows(high, low, th, tl)
    for i, out in enumerate(outs):
        lanes = 2 * i * span // LANES * LANES
        out[4 * span :] = tail[:8, lanes : lanes + LANES]
    for load in loads[PIECES // 2 :]:
        load.wait()


def coarse_rest_kernel(axis, groups, bh_ref, bl_ref, th_ref, tl_ref, table_ref, taps_ref, xs, *rest):
    lots = 1 + groups
    outs, (ys, bs) = rest[:lots], rest[lots:]
    span = 2 * LANES // groups
    rows = xs.shape[0] - 2 * PAD
    taps = taps_ref[...]
    block = 64
    origin = rows // 2 - 16
    filter_rows(xs, ys, None, taps, origin, 16, origin)
    for base in range(rows // 2, rows, block):
        filter_rows(xs, ys, bs, taps, base, block, origin)
    high, low = [pick_rows(table_ref, half, axis, groups, range(groups)) for half in range(2)]
    bh, bl = split_value(gather_rows(bs, 16, LANES))
    for step, block in enumerate(frame_blocks(span, high, low, bh, bl)):
        out, at = (outs[1 + step], 0) if step != 1 else (outs[2], 2 * span)
        for a in range(2):
            out[at + a * span : at + (a + 1) * span] = block[a]
    near_high, near_low = high[: 2 * span], low[: 2 * span]
    tail = tail_rows(near_high, near_low, th_ref[...], tl_ref[...])
    for out, block in zip((outs[0], outs[2]), frame_blocks(span, near_high, near_low, bh_ref[...], bl_ref[...])):
        for a in range(2):
            out[a * span : (a + 1) * span] = block[a]
        out[out.shape[0] - 8 :] = tail[:8, :LANES]


def coarse_section(signal, coarse_taps, axis, groups, shares):
    length = signal.shape[1]
    taps_count, channels = coarse_taps.shape
    count = length // LANES
    rows = signal.reshape(2, count, LANES).transpose(1, 0, 2).reshape(2 * count, LANES)
    table = jnp.asarray(np.stack(split_table(coarse_table(channels, groups, shares))))
    span = 2 * LANES // groups
    lots = groups // 2 - 1
    first = pl.pallas_call(
        lambda *refs: coarse_kernel(axis, groups, *refs),
        out_shape=[pltpu.VMEM((4 * span + 8, LANES), F32)] * lots
        + [pltpu.VMEM((2 * LANES, 2 * LANES), BF16)] * 2
        + [pltpu.VMEM((16, 2 * LANES), BF16)] * 2
        + [
            pltpu.VMEM((2, 2 * LANES, 2 * LANES), BF16),
            pltpu.VMEM((taps_count, LANES), F32),
            pltpu.VMEM((2 * count + 2 * PAD, LANES), F32),
        ],
        in_specs=[ANY] * 3,
        out_specs=[VMEM] * (lots + 7),
        scratch_shapes=[
            pltpu.VMEM((taps_count, channels), F32),
            pltpu.VMEM((count + PAD, LANES), F32),
            pltpu.VMEM((count, LANES), F32),
            pltpu.VMEM((64 + 2 * PAD, LANES), F32),
            pltpu.VMEM((PAD + 32, LANES), F32),
            pltpu.VMEM((32, LANES), F32),
            pltpu.SemaphoreType.DMA((PIECES + 3,)),
        ],
        compiler_params=PARAMS,
        cost_estimate=COST,
        name="coarse",
    )(in_hbm(rows), in_hbm(coarse_taps), in_hbm(table))
    own, pair, late = [pltpu.VMEM((n * span + m, LANES), F32) for n, m in ((2, 8), (4, 8), (2, 0))]
    second = pl.pallas_call(
        lambda *refs: coarse_rest_kernel(axis, groups, *refs),
        out_shape=[own, late, pair] + [late] * (groups - 2),
        in_specs=[VMEM] * 7,
        out_specs=[VMEM] * (1 + groups),
        scratch_shapes=[
            pltpu.VMEM((count + 16 + PAD, LANES), F32),
            pltpu.VMEM((count + 16, LANES), F32),
        ],
        compiler_params=PARAMS,
        cost_estimate=COST,
        name="coarse_rest",
    )(*[in_vmem(value) for value in first[lots:]])
    return first[:lots], second


def terms(xs, taps, parity, m, a, rows):
    reach = [(g, m - 2 * g - parity) for g in range((m - parity) // 2, -1, -1)]
    height = rows.stop - rows.start
    return [xs[g, a, rows] * tiled(taps[j], height) for g, j in reach if j < len(taps)]


def tiled(tap, height):
    return tap[:height] if height <= 8 else jnp.concatenate([tap] * (height // 8), axis=0)


def add_piece(axis, groups, piece, step, xs):
    span = 2 * LANES // groups
    owner = lax.axis_index(axis) ^ step
    at = (step - 2 if step > 1 else step) * span % LANES
    tail = jnp.transpose(piece[piece.shape[0] - 8 :])[at : at + span]
    for a in range(2):
        xs[owner, a] = xs[owner, a] + piece[a * span : (a + 1) * span]
        xs[owner + 1, a, :, 0:4] = xs[owner + 1, a, :, 0:4] + tail[:, 4 * a : 4 * a + 4]


def fine_start_kernel(axis, groups, shares, taps_ref, near_ref, *refs):
    steps = range(3, groups, 2)
    pieces, (out_ref, xs) = refs[: len(steps)], refs[len(steps) :]
    span = 2 * LANES // groups
    small, per, frames = span // shares, span // (4 * shares), 2 * groups
    xs[...] = near_ref[...]
    for step, piece in zip(steps, pieces):
        add_piece(axis, groups, piece, step, xs)
    for a in range(2):
        for h in range(2):
            phase = 2 * a + h
            taps = [taps_ref[phase, j] for j in range(taps_ref.shape[1])]
            for share in range(shares):
                for part in range(2):
                    at = share * small + (2 * part + h) * per
                    for m in range(frames):
                        value = sum(terms(xs, taps, 0, m, a, slice(at, at + per)))
                        out_ref[share, phase, part, m * per : (m + 1) * per] = value


def fine_kernel(axis, groups, shares, share, taps_ref, table_ref, turn_ref, acc_ref, *refs):
    pieces, (out_hbm, xs, fs, yh, yl, zs, os, sem) = refs[:groups], refs[-8:]
    small = 2 * LANES // (groups * shares)
    per, frames = small // 4, 2 * groups
    me = lax.axis_index(axis)
    for step in range(groups):
        base = 2 * small if step == 1 else 0
        for a in range(2):
            xs[me ^ step, a] = pieces[step][base + a * small : base + (a + 1) * small]
    turns = 2 if per >= 16 else 1
    part_of = per // turns
    height = part_of * frames
    length = height * 4
    high, low = table_ref[0], table_ref[1]
    copies = [
        pltpu.make_async_copy(
            os.at[part, pl.ds(turn * length, length)],
            out_hbm.at[part, pl.ds((share * turns + turn) * length, length)],
            sem.at[2 * turn + part],
        )
        for turn in range(turns)
        for part in range(2)
    ]

    def run(turn):
        top = turn * 4 * height
        for a in range(2):
            for h in range(2):
                phase = 2 * a + h
                taps = [taps_ref[phase, j] for j in range(taps_ref.shape[1])]
                columns = []
                for part in range(2):
                    at = (2 * part + h) * per + turn * part_of
                    rows = slice(at, at + part_of)
                    for m in range(frames):
                        at = m * per + turn * part_of
                        value = sum(terms(xs, taps, 1, m, a, rows), acc_ref[share, phase, part, at : at + part_of])
                        at = m * part_of
                        fs[turn, phase, part, at : at + part_of] = value
                    picked = [fs[turn, phase, part, pl.ds(k, frames, stride=part_of), :] for k in range(part_of)]
                    columns.append(jnp.concatenate(picked, axis=0))
                first, second = split_value(jnp.concatenate(columns, axis=1))
                at = top + phase * height
                yh[at : at + height] = first
                yl[at : at + height] = second
        left, right = yh[top : top + 4 * height], yl[top : top + 4 * height]
        zs[top : top + 4 * height] = dot_nn(left, high) + dot_nn(right, high) + dot_nn(left, low)
        for at in range(0, height, 8):
            z = []
            for phase in range(4):
                row = top + phase * height + at
                real, imag = zs[row : row + 8, :LANES], zs[row : row + 8, LANES:]
                if phase:
                    c, s = turn_ref[phase, 0], turn_ref[phase, 1]
                    real, imag = real * c - imag * s, real * s + imag * c
                z.append((real, imag))
            (ar, ai), (br, bi), (cr, ci), (dr, di) = z
            pr, pi, qr, qi = ar + cr, ai + ci, ar - cr, ai - ci
            ur, ui, vr, vi = br + dr, bi + di, br - dr, bi - di
            reals = (pr + ur, qr + vi, pr - ur, qr - vi)
            imags = (pi + ui, qi - vr, pi - ui, qi + vr)
            for part, values in enumerate((reals, imags)):
                for r, value in enumerate(values):
                    row = turn * length + (at // 8 * 4 + r) * 8
                    os[part, row : row + 8, :] = value
        copies[2 * turn].start()
        copies[2 * turn + 1].start()

    run(0)
    for turn in range(1, turns):
        run(turn)
    for copy in copies:
        copy.wait()


def constants_kernel(table_hbm, turn_hbm, table_ref, turn_ref, sems):
    copies = [
        pltpu.make_async_copy(source, target, sems.at[i])
        for i, (source, target) in enumerate(((table_hbm, table_ref), (turn_hbm, turn_ref)))
    ]
    for copy in copies:
        copy.start()
    for copy in copies:
        copy.wait()


def tables_kernel(axis, groups, taps_ref, *refs):
    steps = [0, 1, *range(2, groups, 2)]
    pieces, (spread_ref, near_ref) = refs[: len(steps)], refs[len(steps) :]
    for phase in range(taps_ref.shape[0]):
        for j in range(taps_ref.shape[1]):
            spread_ref[phase, j] = jnp.broadcast_to(taps_ref[phase, j : j + 1], (8, LANES))
    near_ref[...] = jnp.zeros_like(near_ref)
    for step, piece in zip(steps, pieces):
        add_piece(axis, groups, piece, step, near_ref)


def fine_tables_section(pieces, fine_taps, axis, groups):
    taps_count, fine = fine_taps.shape
    taps = fine_taps.reshape(taps_count, LANES, fine // LANES).transpose(2, 0, 1)
    table, turns = fine_tables(fine)
    turns = np.repeat(turns[:, :, None, :], 8, axis=2)
    shape = (fine // LANES, taps_count, 8, LANES)
    constants = pl.pallas_call(
        constants_kernel,
        out_shape=[pltpu.VMEM((2, 2 * LANES, 2 * LANES), BF16), pltpu.VMEM(turns.shape, F32)],
        in_specs=[ANY] * 2,
        out_specs=[VMEM] * 2,
        scratch_shapes=[pltpu.SemaphoreType.DMA((2,))],
        compiler_params=PARAMS,
        cost_estimate=COST,
        name="constants",
    )(in_hbm(jnp.asarray(np.stack(split_table(table)))), in_hbm(jnp.asarray(turns)))
    spread, near = pl.pallas_call(
        lambda *refs: tables_kernel(axis, groups, *refs),
        out_shape=[pltpu.VMEM(shape, F32), pltpu.VMEM((groups + 1, 2, 2 * LANES // groups, LANES), F32)],
        in_specs=[VMEM] * (1 + len(pieces)),
        out_specs=[VMEM] * 2,
        compiler_params=PARAMS,
        cost_estimate=COST,
        name="tables",
    )(in_vmem(taps), *map(in_vmem, pieces))
    return [spread, *constants, near]


def fine_begin(pieces, near, taps, axis, groups, shares):
    span = 2 * LANES // groups
    per, frames = span // (4 * shares), 2 * groups
    acc = pl.pallas_call(
        lambda *refs: fine_start_kernel(axis, groups, shares, *refs),
        out_shape=pltpu.VMEM((shares, 4, 2, frames * per, LANES), F32),
        in_specs=[VMEM] * (2 + len(pieces)),
        out_specs=VMEM,
        scratch_shapes=[pltpu.VMEM((groups + 1, 2, span, LANES), F32)],
        compiler_params=PARAMS,
        cost_estimate=COST,
        name="fine_start",
    )(in_vmem(taps), in_vmem(near), *[in_vmem(value) for value in pieces])
    return acc


def fine_section(moved, tables, acc, axis, groups, shares):
    small = 2 * LANES // (groups * shares)
    per, frames = small // 4, 2 * groups
    height = 4 * frames * per
    length = per * frames * 4
    shared = [*tables, acc]
    out = None
    for share in range(shares):
        more = [] if out is None else [out]
        out = pl.pallas_call(
            lambda *refs: fine_kernel(axis, groups, shares, share, *refs),
            out_shape=pltpu.HBM((2, shares * length, LANES), F32),
            in_specs=[VMEM] * (4 + groups) + [ANY] * len(more),
            out_specs=ANY,
            scratch_shapes=[
                pltpu.VMEM((groups, 2, small, LANES), F32),
                pltpu.VMEM((2, 4, 2, frames * per, LANES), F32),
                pltpu.VMEM((height, 2 * LANES), BF16),
                pltpu.VMEM((height, 2 * LANES), BF16),
                pltpu.VMEM((height, 2 * LANES), F32),
                pltpu.VMEM((2, length, LANES), F32),
                pltpu.SemaphoreType.DMA((4,)),
            ],
            input_output_aliases={4 + groups: 0} if more else {},
            compiler_params=PARAMS,
            cost_estimate=COST,
            name="fine",
        )(*[in_vmem(value) for value in shared + list(moved[share])], *more)
    out = out.reshape(2, shares * per, frames // 8, 4, 8, LANES).transpose(0, 1, 2, 4, 3, 5)
    return out.reshape(2, shares * per, frames, 4 * LANES)


def solution(mesh):
    axis = "tm"
    groups = mesh.shape[axis]

    def swap(value, step):
        return lax.ppermute(value, axis, [(i, i ^ step) for i in range(groups)])

    def staged(signal, coarse_taps, fine_taps):
        shares = 1
        first, second = coarse_section(signal, coarse_taps, axis, groups, shares)
        reached = [swap(value, 2 * i + 2) for i, value in enumerate(first)]
        late = [swap(second[1 + step], step) for step in range(2, groups)]
        beside = swap(second[2], 1)
        moved = [[second[1], beside] + late]
        relayed = []
        for value in reached:
            half = value[value.shape[0] // 2 - 4 :]
            relayed.append(swap(half, 1))
        *tables, near = fine_tables_section([second[0], beside, *reached], fine_taps, axis, groups)
        acc = fine_begin(relayed, near, tables[0], axis, groups, shares)
        return fine_section(moved, tables, acc, axis, groups, shares)

    return jax.shard_map(
        staged,
        mesh=mesh,
        in_specs=(P(None, ("streams", "tm")), P(), P()),
        out_specs=P(None, "tm", "streams", None),
        check_vma=False,
    )
```
